512 devices in a mesh: section: 8 (over y_lo, x), tp: 16 (over z), dp: 4 (over y_hi, core).
Axes of the slice: x: 4, y: 4 (y_hi: 2, y_lo: 2; y = y_hi * 2 + y_lo), z: 16, core: 2. Of those that a mesh axis runs over, the one named last changes fastest.
Arguments:
- stream: bfloat16 [8, 16, 32, 4096], P('section', 'dp', None, 'tp'), may hold values from -120 to 120
- memory_hidden: bfloat16 [16, 32, 4096], P('dp', 'section', 'tp'), may hold values from -120 to 120
- layer_gain: float32 [8, 4096], P('section'), may hold values from 0.5 to 4
- final_gain: float32 [4096], replicated, may hold values from 0.5 to 4
- query_weight: bfloat16 [8, 4096, 4096], P('section', 'dp', 'tp'), may hold values from -0.09375 to 0.09375
- key_weight: bfloat16 [8, 4096, 4096], P('section', 'dp', 'tp'), may hold values from -0.09375 to 0.09375
- value_weight: bfloat16 [8, 4096, 4096], P('section', 'dp', 'tp'), may hold values from -0.09375 to 0.09375
- cotangent: bfloat16 [8, 16, 32, 4096], P('section', 'dp', None, 'tp'), may hold values from -6 to 6
- encoder_lengths: int32 [16], P('dp'), may hold values from 8 to 32
- decoder_lengths: int32 [16], P('dp'), may hold values from 8 to 32
- assignment: int32 [4, 4], P('dp'), may hold values from 0 to 3, each once within a row
Outputs:
- attention_mix: bfloat16 [8, 16, 32, 4096], P('section', 'dp', None, 'tp')
- stream_grad: bfloat16 [8, 16, 32, 4096], P('section', 'dp', None, 'tp')
- memory_grad: bfloat16 [16, 32, 4096], P('dp', 'section', 'tp')
- query_weight_grad: bfloat16 [8, 4096, 4096], P('section', 'dp', 'tp')
- key_weight_grad: bfloat16 [8, 4096, 4096], P('section', 'dp', 'tp')
- value_weight_grad: bfloat16 [8, 4096, 4096], P('section', 'dp', 'tp')
The draws below stay inside these ranges and needn't reach their ends.
Inputs may be any that keep to these rules, and one draw needn't show every extreme that they name: Each row of assignment is a permutation of 0 to 3.
All inputs are finite; a program needn't handle non-finite values.
Results may differ from the reference program's by a relative error of at most 0.019.
The reference program's roundings to bfloat16 on the way count: a program that leaves them out, or rounds other values in their place, can miss the bound.
Values may be sent and summed in bfloat16 or wider, within the bound.
A program may use at most 64 MiB of HBM per device.

```python
import math
import jax
import jax.numpy as jnp
from jax import lax

D = 4096
HEADS = 64
HEAD_DIM = 64
SEQ = 32
MICRO = 4
SAMPLES = 16
N_SECTION = 8
N_TP = 16
N_DP = 4


def scaled_field(key, extent, rising):
    subkeys = jax.random.split(key, 3)
    row_scale = jnp.exp(jax.random.uniform(subkeys[1], extent[:-1] + (1,), jnp.float32, 0.0, math.log(10.0)))
    if rising:
        position = jnp.arange(extent[-1], dtype=jnp.float32) / (extent[-1] - 1)
        upper = math.log(0.75)
        column_scale = jnp.exp(jax.random.uniform(subkeys[2], (extent[-1],), jnp.float32, math.log(0.3), upper) + math.log(10.0) * position)
        column_scale = jnp.minimum(column_scale, 3.0)
    else:
        column_scale = jnp.exp(jax.random.uniform(subkeys[2], (extent[-1],), jnp.float32, math.log(0.3), math.log(3.0)))
    baseline = jnp.clip(jax.random.normal(subkeys[0], extent, jnp.float32), -4.0, 4.0)
    return (baseline * row_scale * column_scale).astype(jnp.bfloat16)


def gain_field(key, extent, rising):
    lowest, highest = (math.log(0.5), math.log(2.0))
    if rising:
        position = jnp.arange(extent[-1], dtype=jnp.float32) / (extent[-1] - 1)
        base = jax.random.uniform(key, extent, jnp.float32, lowest, highest - math.log(2.0))
        return jnp.exp(base + math.log(2.0) * position)
    return jnp.exp(jax.random.uniform(key, extent, jnp.float32, lowest, highest))


def draw_stream(key, part):
    return scaled_field(jax.random.fold_in(key, 11), (N_SECTION, SAMPLES, SEQ, D), False)


def draw_memory_hidden(key, part):
    return scaled_field(jax.random.fold_in(key, 12), (SAMPLES, SEQ, D), True)


def draw_layer_gain(key, part):
    return gain_field(jax.random.fold_in(key, 13), (N_SECTION, D), False)


def draw_final_gain(key, part):
    return gain_field(jax.random.fold_in(key, 14), (D,), True)


def touch_ends(result, rng, smallest, largest):
    longest = result.shape.index(max(result.shape))
    spots = []
    for shift in (0, 1):
        where = [jax.random.randint(jax.random.fold_in(rng, axis), (), 0, length) for axis, length in enumerate(result.shape)]
        where[longest] = (where[longest] + shift) % result.shape[longest]
        spots.append(tuple(where))
    return result.at[spots[0]].set(smallest).at[spots[1]].set(largest)


def block_levels(own_key, dims, pieces, low, largest):
    level, own = 1.0, jax.random.fold_in(own_key, 6)
    for dim, shards_of in pieces:
        steps = jnp.exp(jax.random.uniform(jax.random.fold_in(own, dim), (shards_of,), jnp.float32, low / len(pieces), largest / len(pieces)))
        level = level * jnp.repeat(steps, dims[dim] // shards_of).reshape([-1 if axis == dim else 1 for axis in range(len(dims))])
    return level


def scatter_about(rng, shape, spread, limit, cuts=(), held_as=jnp.bfloat16):
    result = jax.random.normal(rng, shape, jnp.float32) * spread
    if len(cuts) > 0:
        result = block_levels(rng, shape, cuts, -0.22, 0.18) * result
    return jnp.clip(result, min=-limit, max=limit).astype(held_as)


def setup_inputs(seed: int = 0) -> dict:
    streams_of = jax.random.split(jax.random.key(seed), 12)
    return {
        "stream": draw_stream(jax.random.fold_in(streams_of[11], 71), 0),
        "memory_hidden": draw_memory_hidden(jax.random.fold_in(streams_of[11], 71), 0),
        "layer_gain": draw_layer_gain(jax.random.fold_in(streams_of[11], 71), 0),
        "final_gain": draw_final_gain(jax.random.fold_in(streams_of[11], 71), 0),
        "query_weight": scatter_about(streams_of[4], (N_SECTION, D, HEADS * HEAD_DIM), D ** -0.5, 0.09375, ((0, 8), (1, 4), (2, 16))),
        "key_weight": scatter_about(streams_of[5], (N_SECTION, D, HEADS * HEAD_DIM), D ** -0.5, 0.09375, ((0, 8), (1, 4), (2, 16))),
        "value_weight": scatter_about(streams_of[6], (N_SECTION, D, HEADS * HEAD_DIM), D ** -0.5, 0.09375, ((0, 8), (1, 4), (2, 16))),
        "cotangent": scatter_about(streams_of[7], (N_SECTION, SAMPLES, SEQ, HEADS * HEAD_DIM), 1.0, 6.0, ((0, 8), (1, 4), (3, 16))),
        "encoder_lengths": touch_ends(jax.random.randint(streams_of[8], (SAMPLES,), SEQ // 4, SEQ + 1), jax.random.fold_in(streams_of[8], 1), SEQ // 4, SEQ).astype(jnp.int32),
        "decoder_lengths": touch_ends(jax.random.randint(streams_of[9], (SAMPLES,), SEQ // 4, SEQ + 1), jax.random.fold_in(streams_of[9], 1), SEQ // 4, SEQ).astype(jnp.int32),
        "assignment": jax.vmap(lambda own: jax.random.permutation(own, MICRO))(jax.random.split(streams_of[10], N_DP)).reshape((N_DP, MICRO)).astype(jnp.int32),
    }


EPSILON = 1e-06

def rounded(array):
    return lax.optimization_barrier(array.astype(jnp.bfloat16)).astype(jnp.float32)

def normalize(hidden_in, gain):
    floats = hidden_in.astype(jnp.float32)
    inverse = lax.rsqrt(lax.optimization_barrier(jnp.mean(floats * floats, axis=-1, keepdims=True)) + EPSILON)
    return (floats, inverse, (floats * inverse * gain).astype(jnp.bfloat16))

def norm_backward(floats, inverse, gain, upstream):
    mean_dot = lax.optimization_barrier(jnp.mean(floats * gain * upstream, axis=-1, keepdims=True))
    return inverse * (gain * upstream - floats * (inverse * inverse) * mean_dot)

def attention_core(queries, keys, values, raw_upstream, query_len, key_len):
    span = queries.shape[1]
    score_scale = queries.shape[3] ** (-0.5)
    positions = jnp.arange(span, dtype=jnp.int32)
    key_live = positions[None, :] < key_len[:, None]
    row_live = (positions[None, :] < query_len[:, None]).astype(jnp.float32)[:, :, None, None]
    query_f = queries.astype(jnp.float32)
    key_f = keys.astype(jnp.float32)
    value_f = values.astype(jnp.float32)
    scores = jnp.einsum('bqhe,bkhe->bhqk', query_f, key_f) * score_scale
    scores = jnp.where(key_live[:, None, None, :], scores, -1e+30)
    weights = jax.nn.softmax(scores, axis=-1)
    probs_f = rounded(weights)
    mixture = (jnp.einsum('bhqk,bkhe->bqhe', probs_f, value_f) * row_live).astype(jnp.bfloat16)
    upstream_f = rounded(raw_upstream.astype(jnp.float32) * row_live)
    grad_values = jnp.einsum('bhqk,bqhe->bkhe', probs_f, upstream_f).astype(jnp.bfloat16)
    grad_weights = jnp.einsum('bqhe,bkhe->bhqk', upstream_f, value_f)
    grad_scores = rounded(weights * (grad_weights - lax.optimization_barrier(jnp.sum(grad_weights * weights, axis=-1, keepdims=True))) * score_scale)
    grad_queries = jnp.einsum('bhqk,bkhe->bqhe', grad_scores, key_f).astype(jnp.bfloat16)
    grad_keys = jnp.einsum('bhqk,bqhe->bkhe', grad_scores, query_f).astype(jnp.bfloat16)
    return (mixture, grad_queries, grad_keys, grad_values)

def reference(stream, memory_hidden, layer_gain, final_gain, query_weight, key_weight, value_weight, cotangent, encoder_lengths, decoder_lengths, assignment):
    encoder_count = N_SECTION // 2
    width = HEADS * HEAD_DIM
    group_width = width // N_TP
    token_count = SAMPLES * SEQ
    memory_floats, memory_inverse, memory = normalize(memory_hidden, final_gain)
    chosen = (jnp.arange(N_DP, dtype=jnp.int32)[:, None] * MICRO + assignment).reshape(-1).astype(jnp.int32)
    memory_chosen = memory[chosen]
    decoder_keys = encoder_lengths[chosen]
    memory_accum = jnp.zeros((SAMPLES, SEQ, D), jnp.float32)
    mixtures, stream_grads, query_grads, key_grads, value_grads = ([], [], [], [], [])
    four_dims = (SAMPLES, SEQ, HEADS, HEAD_DIM)
    for layer_index in range(N_SECTION):
        decoder = layer_index >= encoder_count
        floats, inverse, normed = normalize(stream[layer_index], layer_gain[layer_index])
        source = memory_chosen if decoder else normed
        query_len = decoder_lengths if decoder else encoder_lengths
        key_len = decoder_keys if decoder else encoder_lengths
        flat_normed = normed.reshape(token_count, D)
        flat_source = source.reshape(token_count, D)
        queries = jnp.dot(flat_normed, query_weight[layer_index], preferred_element_type=jnp.float32).astype(jnp.bfloat16)
        keys = jnp.dot(flat_source, key_weight[layer_index], preferred_element_type=jnp.float32).astype(jnp.bfloat16)
        values = jnp.dot(flat_source, value_weight[layer_index], preferred_element_type=jnp.float32).astype(jnp.bfloat16)
        mixture, grad_queries, grad_keys, grad_values = attention_core(queries.reshape(four_dims), keys.reshape(four_dims), values.reshape(four_dims), cotangent[layer_index].reshape(four_dims), query_len, key_len)
        mixtures.append(mixture.reshape(SAMPLES, SEQ, width))
        query_groups = grad_queries.reshape(token_count, N_TP, group_width).astype(jnp.float32)
        key_groups = grad_keys.reshape(token_count, N_TP, group_width).astype(jnp.float32)
        value_groups = grad_values.reshape(token_count, N_TP, group_width).astype(jnp.float32)
        query_table = query_weight[layer_index].astype(jnp.float32).reshape(D, N_TP, group_width)
        key_table = key_weight[layer_index].astype(jnp.float32).reshape(D, N_TP, group_width)
        value_table = value_weight[layer_index].astype(jnp.float32).reshape(D, N_TP, group_width)
        partial_value = jnp.einsum('tgh,dgh->gtd', query_groups, query_table)
        source_part = jnp.einsum('tgh,dgh->gtd', key_groups, key_table) + jnp.einsum('tgh,dgh->gtd', value_groups, value_table)
        if decoder:
            memory_accum = memory_accum + lax.optimization_barrier(jnp.sum(source_part, axis=0)).reshape(SAMPLES, SEQ, D)
        else:
            partial_value = partial_value + source_part
        summed = lax.optimization_barrier(jnp.sum(rounded(partial_value), axis=0)).reshape(SAMPLES, SEQ, D)
        stream_grads.append(norm_backward(floats, inverse, layer_gain[layer_index], summed).astype(jnp.bfloat16))
        query_grads.append(jnp.dot(flat_normed.T, grad_queries.reshape(token_count, width), preferred_element_type=jnp.float32).astype(jnp.bfloat16))
        key_grads.append(jnp.dot(flat_source.T, grad_keys.reshape(token_count, width), preferred_element_type=jnp.float32).astype(jnp.bfloat16))
        value_grads.append(jnp.dot(flat_source.T, grad_values.reshape(token_count, width), preferred_element_type=jnp.float32).astype(jnp.bfloat16))
    sample_grad = jnp.zeros((SAMPLES, SEQ, D), jnp.float32).at[chosen].add(memory_accum)
    memory_out = norm_backward(memory_floats, memory_inverse, final_gain, sample_grad).astype(jnp.bfloat16)
    return (jnp.stack(mixtures), jnp.stack(stream_grads), memory_out, jnp.stack(query_grads), jnp.stack(key_grads), jnp.stack(value_grads))
```

```python
import functools

import jax
import jax.numpy as jnp
from jax import lax
from jax.experimental import pallas as pl
from jax.experimental.pallas import tpu as pltpu
from jax.sharding import PartitionSpec as P

MESH = pl.DeviceIdType.MESH
F32 = jnp.float32
BF16 = jnp.bfloat16
EPSILON = 1e-06
HEAD_DIM = 64
N_SECTION = 8
N_TP = 16
N_DP = 4
ROWS = 128
WIDE = 256
HALF = 64
PIECE = 16
FIRST_DECODER = N_SECTION // 2
WAYS = [(0, 0), (1, 0), (0, 1), (1, 1)]


def dot_nn(a, b):
    return lax.dot_general(a, b, (((1,), (0,)), ((), ())), preferred_element_type=F32)


def dot_nt(a, b):
    return lax.dot_general(a, b, (((1,), (1,)), ((), ())), preferred_element_type=F32)


def dot_tn(a, b):
    return lax.dot_general(a, b, (((0,), (0,)), ((), ())), preferred_element_type=F32)


def hops(way):
    return N_TP // 2 if way[0] == way[1] else N_TP // 2 - 1


def body(
    stream, mem, lgain, fgain, wq, wk, wv, cot, enc_len, dec_len, assign,
    mix_o, sg_o, mg_o, dq_o, dk_o, dv_o,
    piece, gat, xm, wf, acc, inv, g_own, g_all, x_all, x_rel, part, rs, dots, rsd, h_out, h_in,
    ag_s, ag_r, wy_s, wy_r, wc_s, wc_r, wr_s, wr_r, m_s, m_r, ex_s, ex_r, rs_s, rs_r, d_s, d_r, h_s, h_r, loc,
):
    s = lax.axis_index("section")
    z = lax.axis_index("tp")
    d = lax.axis_index("dp")
    is_dec = s >= FIRST_DECODER
    src = jnp.where(is_dec, 1, 0)
    core = lax.rem(d, 2)
    chip = lax.div(d, 2)
    mate = d + 1 - 2 * core
    far = lax.rem(d + 2, N_DP)
    far_mate = lax.rem(mate + 2, N_DP)
    right = {"tp": lax.rem(z + 1, N_TP)}
    left = {"tp": lax.rem(z + N_TP - 1, N_TP)}
    around = [right, left]

    def remote(a, b, ss, rr, to):
        return pltpu.make_async_remote_copy(
            src_ref=a, dst_ref=b, send_sem=ss, recv_sem=rr, device_id=to, device_id_type=MESH
        )

    barrier = pltpu.get_barrier_semaphore()
    for to in (right, left, {"dp": mate}, {"dp": far}):
        pl.semaphore_signal(barrier, inc=1, device_id=to, device_id_type=MESH)
    for other in range(1, N_SECTION):
        pl.semaphore_signal(
            barrier, inc=1, device_id={"section": lax.rem(s + other, N_SECTION)}, device_id_type=MESH
        )

    own = [
        pltpu.make_async_copy(stream, gat.at[0, z], loc.at[0]),
        pltpu.make_async_copy(wq, wf.at[0, pl.ds(4 * d, 4)], loc.at[1]),
        pltpu.make_async_copy(wk, wf.at[1, pl.ds(4 * d, 4)], loc.at[2]),
        pltpu.make_async_copy(wv, wf.at[2, pl.ds(4 * d, 4)], loc.at[3]),
    ]
    for c in own[1:]:
        c.start()
    own[0].start()
    piece[...] = jnp.concatenate([mem[n].astype(F32) for n in range(4)], axis=0).astype(BF16)
    pl.semaphore_wait(barrier, N_SECTION + 3)

    def ring(which, way, k):
        direction, chunk = way
        rows = pl.ds(chunk * HALF, HALF)
        back = k - 1 if direction == 0 else 1 - k
        at = lax.rem(z - back + N_TP, N_TP)
        return remote(
            gat.at[which, at, rows], gat.at[which, at, rows],
            ag_s.at[which, direction, chunk, k - 1], ag_r.at[which, direction, chunk, k - 1],
            around[direction],
        )

    def weight_far(w):
        return remote(
            wf.at[w, pl.ds(4 * d, 4)], wf.at[w, pl.ds(4 * d, 4)], wy_s.at[w], wy_r.at[w], {"dp": far}
        )

    def weight_mate(w):
        return remote(
            wf.at[w, pl.ds(4 * d, 4)], wf.at[w, pl.ds(4 * d, 4)], wc_s.at[w], wc_r.at[w], {"dp": mate}
        )

    def weight_relay(w):
        return remote(
            wf.at[w, pl.ds(4 * far, 4)], wf.at[w, pl.ds(4 * far, 4)], wr_s.at[w], wr_r.at[w], {"dp": mate}
        )

    own[0].wait()
    for way in WAYS:
        ring(0, way, 1).start()
    for w in range(3):
        own[1 + w].wait()
        weight_far(w).start()

    def mem_send(i):
        return remote(
            piece, gat.at[1, z, pl.ds(s * PIECE, PIECE)], m_s.at[i], m_r.at[0], {"section": FIRST_DECODER + i}
        )

    def mem_keep():
        return pltpu.make_async_copy(piece, gat.at[1, z, pl.ds(s * PIECE, PIECE)], m_r.at[0])

    for i in range(N_SECTION - FIRST_DECODER):
        @pl.when(s != FIRST_DECODER + i)
        def _():
            mem_send(i).start()

    @pl.when(is_dec)
    def _():
        mem_keep().start()

    for w in range(3):
        weight_mate(w).start()

    @pl.when(is_dec)
    def _():
        pltpu.make_async_copy(gat.at[1, z], gat.at[1, z], m_r.at[0]).wait()
        for way in WAYS:
            ring(1, way, 1).start()

    def ring_step(k, _):
        for which in range(2):
            def go():
                for way in WAYS:
                    ring(which, way, k - 1).wait_recv()
                    if hops(way) == N_TP // 2:
                        ring(which, way, k).start()
                    else:
                        @pl.when(k < N_TP // 2)
                        def _():
                            ring(which, way, k).start()
            if which == 0:
                go()
            else:
                pl.when(is_dec)(go)
        return 0

    lax.fori_loop(2, 6, ring_step, 0)
    weight_far(0).wait_recv()
    weight_relay(0).start()
    lax.fori_loop(6, N_TP // 2 + 1, ring_step, 0)
    for way in WAYS:
        if hops(way) == N_TP // 2:
            ring(0, way, N_TP // 2).wait_recv()

    @pl.when(is_dec)
    def _():
        for way in WAYS:
            if hops(way) == N_TP // 2:
                ring(1, way, N_TP // 2).wait_recv()

    weight_far(1).wait_recv()
    weight_relay(1).start()

    def scaled(which, gain):
        def step(i, total):
            value = gat[which, i].astype(F32)
            wide = gain[0:1, pl.ds(pl.multiple_of(i * WIDE, WIDE), WIDE)]
            xm[which, i] = (value * wide).astype(BF16)
            return total + value * value

        total = lax.fori_loop(0, N_TP, step, jnp.zeros((ROWS, WIDE), F32))
        mean = jnp.sum(total, axis=1, keepdims=True) * (1.0 / (N_TP * WIDE))
        return jnp.broadcast_to(lax.rsqrt(mean + EPSILON), (ROWS, 128))

    stream_inverse = scaled(0, lgain)
    inv[0] = stream_inverse
    inv[1] = stream_inverse

    @pl.when(is_dec)
    def _():
        inv[1] = scaled(1, fgain)

    def project(w, begin, start):
        side = 0 if w == 0 else src

        def step(i, total):
            return total + dot_nn(xm[side, begin + i], wf[w, begin + i])

        acc[w] = lax.fori_loop(0, N_TP // 2, step, start)

    for w in range(3):
        weight_mate(w).wait_recv()
        project(w, chip * (N_TP // 2), jnp.zeros((ROWS, WIDE), F32))
    for w in range(3):
        if w == 2:
            weight_far(2).wait_recv()
            weight_relay(2).start()
        weight_relay(w).wait_recv()
        project(w, (1 - chip) * (N_TP // 2), acc[w])

    def give_far(side):
        return remote(
            xm.at[side, pl.ds(4 * far, 4)], x_all.at[side, :, d], ex_s.at[side, 0], ex_r.at[side, 0], {"dp": far}
        )

    def give_far_mate(side):
        return remote(
            xm.at[side, pl.ds(4 * far_mate, 4)], x_rel.at[side], ex_s.at[side, 1], ex_r.at[side, 1], {"dp": far}
        )

    def give_mate(side):
        return remote(
            xm.at[side, pl.ds(4 * mate, 4)], x_all.at[side, :, d], ex_s.at[side, 2], ex_r.at[side, 2], {"dp": mate}
        )

    def relay_mate(side):
        return remote(
            x_rel.at[side], x_all.at[side, :, far], ex_s.at[side, 3], ex_r.at[side, 3], {"dp": mate}
        )

    def keep_own(side):
        return pltpu.make_async_copy(xm.at[side, pl.ds(4 * d, 4)], x_all.at[side, :, d], loc.at[4 + side])

    def start_exchange(side):
        give_far_mate(side).start()
        give_far(side).start()
        give_mate(side).start()
        keep_own(side).start()

    start_exchange(0)

    @pl.when(is_dec)
    def _():
        start_exchange(1)

    row = lax.broadcasted_iota(jnp.int32, (ROWS, ROWS), 0)
    col = lax.broadcasted_iota(jnp.int32, (ROWS, ROWS), 1)
    row_sample = lax.shift_right_logical(row, 5)
    col_sample = jnp.where(
        is_dec, jnp.bitwise_and(lax.shift_right_logical(col, 2), 3), lax.shift_right_logical(col, 5)
    )
    col_slot = jnp.where(
        is_dec, lax.shift_right_logical(col, 4) * 4 + jnp.bitwise_and(col, 3), jnp.bitwise_and(col, 31)
    )
    wanted = jnp.zeros((ROWS, ROWS), jnp.int32)
    key_len = jnp.zeros((ROWS, ROWS), jnp.int32)
    query_len = jnp.zeros((ROWS, ROWS), jnp.int32)
    for m in range(4):
        chosen = jnp.where(is_dec, assign[m], m)
        length = jnp.where(is_dec, dec_len[m], enc_len[m])
        wanted = jnp.where(row_sample == m, chosen, wanted)
        key_len = jnp.where(col_sample == m, enc_len[m], key_len)
        query_len = jnp.where(row_sample == m, length, query_len)
    live = jnp.logical_and(wanted == col_sample, col_slot < key_len)
    row_live = (jnp.bitwise_and(row, 31) < query_len).astype(F32)[:, 0:HEAD_DIM]

    q_scale = jnp.concatenate([inv[0], inv[0]], axis=1)
    s_scale = jnp.concatenate([inv[1], inv[1]], axis=1)
    queries = (acc[0] * q_scale).astype(BF16)
    keys = (acc[1] * s_scale).astype(BF16)
    values = (acc[2] * s_scale).astype(BF16)
    scale = HEAD_DIM**-0.5
    for h in range(WIDE // HEAD_DIM):
        at = slice(h * HEAD_DIM, (h + 1) * HEAD_DIM)
        qh, kh, vh = queries[:, at], keys[:, at], values[:, at]
        scores = jnp.where(live, dot_nt(qh, kh) * scale, -1e30)
        raised = jnp.exp(scores - jnp.max(scores, axis=1, keepdims=True))
        weights = raised / jnp.sum(raised, axis=1, keepdims=True)
        probs = weights.astype(BF16)
        mix_o[:, at] = (dot_nn(probs, vh) * row_live).astype(BF16)
        upstream = (cot[:, at].astype(F32) * row_live).astype(BF16)
        grad_weights = dot_nt(upstream, vh)
        inner = jnp.sum(grad_weights * weights, axis=1, keepdims=True)
        grad_scores = (weights * (grad_weights - inner) * scale).astype(BF16)
        g_own[0, :, at] = (dot_nn(grad_scores, kh) * inv[0][:, 0:HEAD_DIM]).astype(BF16)
        g_own[1, :, at] = (dot_tn(grad_scores, qh) * inv[1][:, 0:HEAD_DIM]).astype(BF16)
        g_own[2, :, at] = (dot_tn(probs, upstream) * inv[1][:, 0:HEAD_DIM]).astype(BF16)

    shared_dot = g_own[1].astype(F32) * acc[1] + g_own[2].astype(F32) * acc[2]
    query_dot = g_own[0].astype(F32) * acc[0]
    diagonal = row == col
    for side, total in ((0, jnp.where(is_dec, query_dot, query_dot + shared_dot)), (1, shared_dot)):
        column = jnp.sum(total, axis=1, keepdims=True) * (1.0 / (N_TP * WIDE)) * inv[side] * inv[side]
        across = jnp.sum(jnp.where(diagonal, column, 0.0), axis=0, keepdims=True)
        dots[:, side * 128 : (side + 1) * 128] = jnp.broadcast_to(across, (8, 128))

    def back(i):
        grad_q = dot_nt(g_own[0], wf[0, i])
        grad_s = dot_nt(g_own[1], wf[1, i]) + dot_nt(g_own[2], wf[2, i])
        part[0, i] = jnp.where(is_dec, grad_q, grad_q + grad_s).astype(BF16)
        part[1, i] = grad_s.astype(BF16)

    def chain_at(way_hops, direction, k):
        ahead = way_hops + 1 - k
        return lax.rem(z + ahead, N_TP) if direction == 0 else lax.rem(z - ahead + N_TP, N_TP)

    def chain(side, way, k, first):
        direction, chunk = way
        rows = pl.ds(chunk * HALF, HALF)
        begin = (
            part.at[side, chain_at(hops(way), direction, k), rows] if first else rs.at[side, direction, k - 2, rows]
        )
        return remote(
            begin, rs.at[side, direction, k - 1, rows],
            rs_s.at[side, direction, chunk, k - 1], rs_r.at[side, direction, chunk, k - 1], around[direction],
        )

    def chain_dots(direction, k, first):
        begin = dots if first else rsd.at[direction, k - 2]
        return remote(begin, rsd.at[direction, k - 1], d_s.at[direction, k - 1], d_r.at[direction, k - 1], around[direction])

    half = N_TP // 2
    back(lax.rem(z + half, N_TP))
    back(lax.rem(z + half - 1, N_TP))
    back(lax.rem(z + half + 1, N_TP))

    def chain_first(side):
        for way in WAYS:
            chain(side, way, 1, True).start()

    @pl.when(is_dec)
    def _():
        chain_first(1)

    chain_first(0)
    chain_dots(0, 1, True).start()
    chain_dots(1, 1, True).start()

    def g_far():
        return remote(g_own, g_all.at[:, d], ex_s.at[2, 0], ex_r.at[2, 0], {"dp": far})

    def g_mate():
        return remote(g_own, g_all.at[:, d], ex_s.at[2, 2], ex_r.at[2, 2], {"dp": mate})

    def g_relay():
        return remote(g_all.at[:, far], g_all.at[:, far], ex_s.at[2, 3], ex_r.at[2, 3], {"dp": mate})

    g_keep = pltpu.make_async_copy(g_own, g_all.at[:, d], loc.at[6])
    g_far().start()
    g_mate().start()
    g_keep.start()

    def chain_step(k, _):
        back(lax.rem(z + half - k, N_TP))

        @pl.when(k < half)
        def _():
            back(lax.rem(z + half + k, N_TP))

        def go(side):
            for way in WAYS:
                direction, chunk = way
                last = hops(way)

                def one():
                    chain(side, way, k - 1, True).wait_recv()
                    rows = pl.ds(chunk * HALF, HALF)
                    target = chain_at(last, direction, k)
                    rs[side, direction, k - 2, rows] = (
                        rs[side, direction, k - 2, rows].astype(F32) + part[side, target, rows].astype(F32)
                    ).astype(BF16)
                    chain(side, way, k, False).start()

                if last == N_TP // 2:
                    one()
                else:
                    pl.when(k < N_TP // 2)(one)

        pl.when(is_dec)(lambda: go(1))
        go(0)
        for direction in range(2):
            def one_dots():
                chain_dots(direction, k - 1, True).wait_recv()
                rsd[direction, k - 2] = rsd[direction, k - 2] + dots[...]
                chain_dots(direction, k, False).start()

            if direction == 0:
                one_dots()
            else:
                pl.when(k < N_TP // 2)(one_dots)
        return 0

    def relay(side):
        give_far_mate(side).wait_recv()
        relay_mate(side).start()

    def settled(side):
        give_far(side).wait_recv()
        give_mate(side).wait_recv()
        relay_mate(side).wait_recv()
        keep_own(side).wait()

    def weight_gradient(w, side, out):
        for j in range(4):
            left_side = x_all[side, j].reshape(N_DP * ROWS, WIDE)
            right_side = g_all[w].reshape(N_DP * ROWS, WIDE)
            out[j] = dot_tn(left_side, right_side).astype(BF16)

    lax.fori_loop(2, 6, chain_step, 0)
    g_far().wait_recv()
    g_relay().start()
    relay(0)
    lax.fori_loop(6, 8, chain_step, 0)
    pl.when(is_dec)(lambda: relay(1))
    settled(0)
    g_mate().wait_recv()
    g_relay().wait_recv()
    g_keep.wait()
    weight_gradient(0, 0, dq_o)
    lax.fori_loop(8, N_TP // 2 + 1, chain_step, 0)
    chain_dots(0, N_TP // 2, True).wait_recv()
    chain_dots(1, N_TP // 2 - 1, True).wait_recv()
    summed = rsd[0, N_TP // 2 - 1] + rsd[1, N_TP // 2 - 2] + dots[...]

    def arrived(side, chunk):
        rows = pl.ds(chunk * HALF, HALF)
        total = part[side, z, rows].astype(F32)
        for direction in range(2):
            way = (direction, chunk)
            chain(side, way, hops(way), True).wait_recv()
            total = total + rs[side, direction, hops(way) - 1, rows].astype(F32)
        return total

    def column_of(side):
        across = jnp.broadcast_to(summed[0:1, side * 128 : (side + 1) * 128], (ROWS, ROWS))
        return jnp.sum(jnp.where(diagonal, across, 0.0), axis=1, keepdims=True)

    here = pl.ds(pl.multiple_of(z * WIDE, WIDE), WIDE)

    def give_memory(i):
        return remote(h_out.at[i], h_in.at[s - FIRST_DECODER], h_s.at[i], h_r.at[0], {"section": i})

    @pl.when(is_dec)
    def _():
        gain = fgain[0:1, here]
        column = column_of(1)
        for chunk in range(2):
            rows = slice(chunk * HALF, (chunk + 1) * HALF)
            value = gain * arrived(1, chunk) - gat[1, z, rows].astype(F32) * column[rows]
            h_out[chunk * 4 : chunk * 4 + 4] = value.reshape(4, PIECE, WIDE)
        for i in range(N_SECTION):
            @pl.when(s != i)
            def _():
                give_memory(i).start()
        pltpu.make_async_copy(h_out.at[s], h_in.at[s - FIRST_DECODER], h_r.at[0]).start()

    gain_here = lgain[0:1, here]
    stream_column = column_of(0)
    for chunk in range(2):
        rows = slice(chunk * HALF, (chunk + 1) * HALF)
        value = gain_here * arrived(0, chunk) - stream[rows].astype(F32) * stream_column[rows]
        sg_o[rows] = value.astype(BF16)

    pl.when(is_dec)(lambda: settled(1))
    weight_gradient(1, src, dk_o)
    weight_gradient(2, src, dv_o)

    pltpu.make_async_copy(h_in, h_in, h_r.at[0]).wait()
    mg_o[...] = h_in[0] + h_in[1] + h_in[2] + h_in[3]

    def drain(which):
        for way in WAYS:
            def step(k, _):
                ring(which, way, k).wait_send()
                chain(which, way, k, True).wait_send()
                return 0

            lax.fori_loop(1, hops(way) + 1, step, 0)

    drain(0)
    pl.when(is_dec)(lambda: drain(1))
    for w in range(3):
        weight_far(w).wait_send()
        weight_mate(w).wait_send()
        weight_relay(w).wait_send()
    for i in range(N_SECTION - FIRST_DECODER):
        @pl.when(s != FIRST_DECODER + i)
        def _():
            mem_send(i).wait_send()

    def drain_exchange(side):
        give_far(side).wait_send()
        give_far_mate(side).wait_send()
        give_mate(side).wait_send()
        relay_mate(side).wait_send()

    drain_exchange(0)
    pl.when(is_dec)(lambda: drain_exchange(1))
    g_far().wait_send()
    g_mate().wait_send()
    g_relay().wait_send()
    for direction in range(2):
        def step(k, _):
            chain_dots(direction, k, True).wait_send()
            return 0

        lax.fori_loop(1, N_TP // 2 + 1 - direction, step, 0)

    @pl.when(is_dec)
    def _():
        for i in range(N_SECTION):
            @pl.when(s != i)
            def _():
                give_memory(i).wait_send()


def hand_out(mix, sg, mg, dq, dk, dv, mix_o, sg_o, mg_o, dq_o, dk_o, dv_o):
    mix_o[...] = mix[...]
    sg_o[...] = sg[...]
    for n in range(4):
        mg_o[n] = mg[n * 4 : n * 4 + 4].astype(BF16)
    dq_o[...] = dq[...]
    dk_o[...] = dk[...]
    dv_o[...] = dv[...]


def shards(
    stream, memory_hidden, layer_gain, final_gain, query_weight, key_weight, value_weight,
    cotangent, encoder_lengths, decoder_lengths, assignment,
):
    vmem = pl.BlockSpec(memory_space=pltpu.VMEM)
    hbm = pl.BlockSpec(memory_space=pl.ANY)
    smem = pl.BlockSpec(memory_space=pltpu.SMEM)
    dma = pltpu.SemaphoreType.DMA
    outs = pl.pallas_call(
        body,
        name="relay",
        out_shape=(
            jax.ShapeDtypeStruct((ROWS, WIDE), BF16),
            jax.ShapeDtypeStruct((ROWS, WIDE), BF16),
            jax.ShapeDtypeStruct((PIECE, WIDE), F32),
            jax.ShapeDtypeStruct((4, WIDE, WIDE), BF16),
            jax.ShapeDtypeStruct((4, WIDE, WIDE), BF16),
            jax.ShapeDtypeStruct((4, WIDE, WIDE), BF16),
        ),
        in_specs=[vmem, vmem, vmem, vmem, hbm, hbm, hbm, vmem, smem, smem, smem],
        out_specs=(vmem,) * 6,
        scratch_shapes=[
            pltpu.VMEM((PIECE, WIDE), BF16),
            pltpu.VMEM((2, N_TP, ROWS, WIDE), BF16),
            pltpu.VMEM((2, N_TP, ROWS, WIDE), BF16),
            pltpu.VMEM((3, N_TP, WIDE, WIDE), BF16),
            pltpu.VMEM((3, ROWS, WIDE), F32),
            pltpu.VMEM((2, ROWS, 128), F32),
            pltpu.VMEM((3, ROWS, WIDE), BF16),
            pltpu.VMEM((3, N_DP, ROWS, WIDE), BF16),
            pltpu.VMEM((2, 4, N_DP, ROWS, WIDE), BF16),
            pltpu.VMEM((2, 4, ROWS, WIDE), BF16),
            pltpu.VMEM((2, N_TP, ROWS, WIDE), BF16),
            pltpu.VMEM((2, 2, N_TP // 2, ROWS, WIDE), BF16),
            pltpu.VMEM((8, 256), F32),
            pltpu.VMEM((2, N_TP // 2, 8, 256), F32),
            pltpu.VMEM((N_SECTION, PIECE, WIDE), F32),
            pltpu.VMEM((N_SECTION - FIRST_DECODER, PIECE, WIDE), F32),
            dma((2, 2, 2, 8)), dma((2, 2, 2, 8)),
            dma((3,)), dma((3,)), dma((3,)), dma((3,)), dma((3,)), dma((3,)),
            dma((4,)), dma((1,)),
            dma((3, 4)), dma((3, 4)),
            dma((2, 2, 2, 8)), dma((2, 2, 2, 8)),
            dma((2, 8)), dma((2, 8)),
            dma((8,)), dma((1,)),
            dma((7,)),
        ],
        compiler_params=pltpu.CompilerParams(
            collective_id=0, has_side_effects=True, vmem_limit_bytes=60 * 1024 * 1024
        ),
    )(
        stream.reshape(ROWS, WIDE),
        memory_hidden,
        layer_gain,
        final_gain.reshape(1, N_TP * WIDE),
        query_weight.reshape(4, WIDE, WIDE),
        key_weight.reshape(4, WIDE, WIDE),
        value_weight.reshape(4, WIDE, WIDE),
        cotangent.reshape(ROWS, WIDE),
        encoder_lengths,
        decoder_lengths,
        assignment.reshape(4),
    )
    mixture, stream_grad, memory_grad, dq, dk, dv = pl.pallas_call(
        hand_out,
        name="hand_out",
        out_shape=(
            jax.ShapeDtypeStruct((ROWS, WIDE), BF16),
            jax.ShapeDtypeStruct((ROWS, WIDE), BF16),
            jax.ShapeDtypeStruct((4, 4, WIDE), BF16),
            jax.ShapeDtypeStruct((4, WIDE, WIDE), BF16),
            jax.ShapeDtypeStruct((4, WIDE, WIDE), BF16),
            jax.ShapeDtypeStruct((4, WIDE, WIDE), BF16),
        ),
        in_specs=[vmem] * 6,
        out_specs=(vmem,) * 6,
    )(*outs)
    rows = (1, 4, 32, WIDE)
    square = (1, 4 * WIDE, WIDE)
    return (
        mixture.reshape(rows),
        stream_grad.reshape(rows),
        memory_grad,
        dq.reshape(square),
        dk.reshape(square),
        dv.reshape(square),
    )


def solution(mesh):
    tokens = P("section", "dp", None, "tp")
    weight = P("section", "dp", "tp")
    memory = P("dp", "section", "tp")
    return jax.shard_map(
        shards,
        mesh=mesh,
        in_specs=(
            tokens, memory, P("section", None), P(), weight, weight, weight, tokens, P("dp"), P("dp"), P("dp", None),
        ),
        out_specs=(tokens, tokens, memory, weight, weight, weight),
        check_vma=False,
    )
```

```python
import functools

import jax
import jax.numpy as jnp
from jax import lax
from jax.experimental import pallas as pl
from jax.experimental.pallas import tpu as pltpu
from jax.sharding import PartitionSpec as P

MESH = pl.DeviceIdType.MESH
F32 = jnp.float32
BF16 = jnp.bfloat16
EPSILON = 1e-06
HEAD_DIM = 64
N_SECTION = 8
N_TP = 16
N_DP = 4
ROWS = 128
WIDE = 256
HALF = 64
PIECE = 16
FIRST_DECODER = N_SECTION // 2
WAYS = [(0, 0), (1, 0), (0, 1), (1, 1)]


def dot_nn(a, b):
    return lax.dot_general(a, b, (((1,), (0,)), ((), ())), preferred_element_type=F32)


def dot_nt(a, b):
    return lax.dot_general(a, b, (((1,), (1,)), ((), ())), preferred_element_type=F32)


def dot_tn(a, b):
    return lax.dot_general(a, b, (((0,), (0,)), ((), ())), preferred_element_type=F32)


def hops(way):
    return N_TP // 2 if way[0] == way[1] else N_TP // 2 - 1


def body(
    stream, mem, lgain, fgain, wq, wk, wv, cot, enc_len, dec_len, assign,
    mix_o, sg_o, mg_o, dq_o, dk_o, dv_o,
    piece, gat, xm, wf, acc, inv, g_own, g_all, x_all, x_rel, part, rs, dots, rsd, h_out, h_in,
    ag_s, ag_r, wy_s, wy_r, wc_s, wc_r, wr_s, wr_r, m_s, m_r, ex_s, ex_r, rs_s, rs_r, d_s, d_r, h_s, h_r, loc,
):
    s = lax.axis_index("section")
    z = lax.axis_index("tp")
    d = lax.axis_index("dp")
    is_dec = s >= FIRST_DECODER
    src = jnp.where(is_dec, 1, 0)
    core = lax.rem(d, 2)
    chip = lax.div(d, 2)
    mate = d + 1 - 2 * core
    far = lax.rem(d + 2, N_DP)
    far_mate = lax.rem(mate + 2, N_DP)
    right = {"tp": lax.rem(z + 1, N_TP)}
    left = {"tp": lax.rem(z + N_TP - 1, N_TP)}
    around = [right, left]

    def remote(a, b, ss, rr, to):
        return pltpu.make_async_remote_copy(
            src_ref=a, dst_ref=b, send_sem=ss, recv_sem=rr, device_id=to, device_id_type=MESH
        )

    barrier = pltpu.get_barrier_semaphore()
    for to in (right, left, {"dp": mate}, {"dp": far}):
        pl.semaphore_signal(barrier, inc=1, device_id=to, device_id_type=MESH)
    for other in range(1, N_SECTION):
        pl.semaphore_signal(
            barrier, inc=1, device_id={"section": lax.rem(s + other, N_SECTION)}, device_id_type=MESH
        )

    own = [
        pltpu.make_async_copy(stream, gat.at[0, z], loc.at[0]),
        pltpu.make_async_copy(wq, wf.at[0, pl.ds(4 * d, 4)], loc.at[1]),
        pltpu.make_async_copy(wk, wf.at[1, pl.ds(4 * d, 4)], loc.at[2]),
        pltpu.make_async_copy(wv, wf.at[2, pl.ds(4 * d, 4)], loc.at[3]),
    ]
    for c in own[1:]:
        c.start()
    own[0].start()
    piece[...] = jnp.concatenate([mem[n].astype(F32) for n in range(4)], axis=0).astype(BF16)
    pl.semaphore_wait(barrier, N_SECTION + 3)

    def ring(which, way, k):
        direction, chunk = way
        rows = pl.ds(chunk * HALF, HALF)
        back = k - 1 if direction == 0 else 1 - k
        at = lax.rem(z - back + N_TP, N_TP)
        return remote(
            gat.at[which, at, rows], gat.at[which, at, rows],
            ag_s.at[which, direction, chunk, k - 1], ag_r.at[which, direction, chunk, k - 1],
            around[direction],
        )

    def weight_far(w):
        return remote(
            wf.at[w, pl.ds(4 * d, 4)], wf.at[w, pl.ds(4 * d, 4)], wy_s.at[w], wy_r.at[w], {"dp": far}
        )

    def weight_mate(w):
        return remote(
            wf.at[w, pl.ds(4 * d, 4)], wf.at[w, pl.ds(4 * d, 4)], wc_s.at[w], wc_r.at[w], {"dp": mate}
        )

    def weight_relay(w):
        return remote(
            wf.at[w, pl.ds(4 * far, 4)], wf.at[w, pl.ds(4 * far, 4)], wr_s.at[w], wr_r.at[w], {"dp": mate}
        )

    def mem_send(i):
        return remote(
            piece, gat.at[1, z, pl.ds(s * PIECE, PIECE)], m_s.at[i], m_r.at[0], {"section": FIRST_DECODER + i}
        )

    def mem_keep():
        return pltpu.make_async_copy(piece, gat.at[1, z, pl.ds(s * PIECE, PIECE)], m_r.at[0])

    for i in range(N_SECTION - FIRST_DECODER):
        @pl.when(s != FIRST_DECODER + i)
        def _():
            mem_send(i).start()

    @pl.when(is_dec)
    def _():
        mem_keep().start()

    own[0].wait()
    for way in WAYS:
        ring(0, way, 1).start()
    for w in range(3):
        own[1 + w].wait()
        weight_far(w).start()

    for w in range(3):
        weight_mate(w).start()

    @pl.when(is_dec)
    def _():
        pltpu.make_async_copy(gat.at[1, z], gat.at[1, z], m_r.at[0]).wait()
        for way in WAYS:
            ring(1, way, 1).start()

    def ring_step(k, _):
        for which in range(2):
            def go():
                for way in WAYS:
                    ring(which, way, k - 1).wait_recv()
                    if hops(way) == N_TP // 2:
                        ring(which, way, k).start()
                    else:
                        @pl.when(k < N_TP // 2)
                        def _():
                            ring(which, way, k).start()
            if which == 0:
                go()
            else:
                pl.when(is_dec)(go)
        return 0

    lax.fori_loop(2, 6, ring_step, 0)
    weight_far(0).wait_recv()
    weight_relay(0).start()
    lax.fori_loop(6, N_TP // 2 + 1, ring_step, 0)
    for way in WAYS:
        if hops(way) == N_TP // 2:
            ring(0, way, N_TP // 2).wait_recv()

    @pl.when(is_dec)
    def _():
        for way in WAYS:
            if hops(way) == N_TP // 2:
                ring(1, way, N_TP // 2).wait_recv()

    weight_far(1).wait_recv()
    weight_relay(1).start()

    def scaled(which, gain):
        def step(i, total):
            value = gat[which, i].astype(F32)
            wide = gain[0:1, pl.ds(pl.multiple_of(i * WIDE, WIDE), WIDE)]
            xm[which, i] = (value * wide).astype(BF16)
            return total + value * value

        total = lax.fori_loop(0, N_TP, step, jnp.zeros((ROWS, WIDE), F32))
        mean = jnp.sum(total, axis=1, keepdims=True) * (1.0 / (N_TP * WIDE))
        return jnp.broadcast_to(lax.rsqrt(mean + EPSILON), (ROWS, 128))

    stream_inverse = scaled(0, lgain)
    inv[0] = stream_inverse
    inv[1] = stream_inverse

    @pl.when(is_dec)
    def _():
        inv[1] = scaled(1, fgain)

    def project(w, begin, start):
        side = 0 if w == 0 else src

        def step(i, total):
            return total + dot_nn(xm[side, begin + i], wf[w, begin + i])

        acc[w] = lax.fori_loop(0, N_TP // 2, step, start)

    for w in range(3):
        weight_mate(w).wait_recv()
        project(w, chip * (N_TP // 2), jnp.zeros((ROWS, WIDE), F32))
    for w in range(3):
        if w == 2:
            weight_far(2).wait_recv()
            weight_relay(2).start()
        weight_relay(w).wait_recv()
        project(w, (1 - chip) * (N_TP // 2), acc[w])

    def give_far(side):
        return remote(
            xm.at[side, pl.ds(4 * far, 4)], x_all.at[side, :, d], ex_s.at[side, 0], ex_r.at[side, 0], {"dp": far}
        )

    def give_far_mate(side):
        return remote(
            xm.at[side, pl.ds(4 * far_mate, 4)], x_rel.at[side], ex_s.at[side, 1], ex_r.at[side, 1], {"dp": far}
        )

    def give_mate(side):
        return remote(
            xm.at[side, pl.ds(4 * mate, 4)], x_all.at[side, :, d], ex_s.at[side, 2], ex_r.at[side, 2], {"dp": mate}
        )

    def relay_mate(side):
        return remote(
            x_rel.at[side], x_all.at[side, :, far], ex_s.at[side, 3], ex_r.at[side, 3], {"dp": mate}
        )

    def keep_own(side):
        return pltpu.make_async_copy(xm.at[side, pl.ds(4 * d, 4)], x_all.at[side, :, d], loc.at[4 + side])

    def start_exchange(side):
        give_far_mate(side).start()
        give_far(side).start()
        give_mate(side).start()
        keep_own(side).start()

    start_exchange(0)

    @pl.when(is_dec)
    def _():
        start_exchange(1)

    row = lax.broadcasted_iota(jnp.int32, (ROWS, ROWS), 0)
    col = lax.broadcasted_iota(jnp.int32, (ROWS, ROWS), 1)
    row_sample = lax.shift_right_logical(row, 5)
    col_sample = jnp.where(
        is_dec, jnp.bitwise_and(lax.shift_right_logical(col, 2), 3), lax.shift_right_logical(col, 5)
    )
    col_slot = jnp.where(
        is_dec, lax.shift_right_logical(col, 4) * 4 + jnp.bitwise_and(col, 3), jnp.bitwise_and(col, 31)
    )
    wanted = jnp.zeros((ROWS, ROWS), jnp.int32)
    key_len = jnp.zeros((ROWS, ROWS), jnp.int32)
    query_len = jnp.zeros((ROWS, ROWS), jnp.int32)
    for m in range(4):
        chosen = jnp.where(is_dec, assign[m], m)
        length = jnp.where(is_dec, dec_len[m], enc_len[m])
        wanted = jnp.where(row_sample == m, chosen, wanted)
        key_len = jnp.where(col_sample == m, enc_len[m], key_len)
        query_len = jnp.where(row_sample == m, length, query_len)
    live = jnp.logical_and(wanted == col_sample, col_slot < key_len)
    row_live = (jnp.bitwise_and(row, 31) < query_len).astype(F32)[:, 0:HEAD_DIM]

    q_scale = jnp.concatenate([inv[0], inv[0]], axis=1)
    s_scale = jnp.concatenate([inv[1], inv[1]], axis=1)
    queries = (acc[0] * q_scale).astype(BF16)
    keys = (acc[1] * s_scale).astype(BF16)
    values = (acc[2] * s_scale).astype(BF16)
    scale = HEAD_DIM**-0.5
    for h in range(WIDE // HEAD_DIM):
        at = slice(h * HEAD_DIM, (h + 1) * HEAD_DIM)
        qh, kh, vh = queries[:, at], keys[:, at], values[:, at]
        scores = jnp.where(live, dot_nt(qh, kh) * scale, -1e30)
        raised = jnp.exp(scores - jnp.max(scores, axis=1, keepdims=True))
        weights = raised / jnp.sum(raised, axis=1, keepdims=True)
        probs = weights.astype(BF16)
        mix_o[:, at] = (dot_nn(probs, vh) * row_live).astype(BF16)
        upstream = (cot[:, at].astype(F32) * row_live).astype(BF16)
        grad_weights = dot_nt(upstream, vh)
        inner = jnp.sum(grad_weights * weights, axis=1, keepdims=True)
        grad_scores = (weights * (grad_weights - inner) * scale).astype(BF16)
        g_own[0, :, at] = (dot_nn(grad_scores, kh) * inv[0][:, 0:HEAD_DIM]).astype(BF16)
        g_own[1, :, at] = (dot_tn(grad_scores, qh) * inv[1][:, 0:HEAD_DIM]).astype(BF16)
        g_own[2, :, at] = (dot_tn(probs, upstream) * inv[1][:, 0:HEAD_DIM]).astype(BF16)

    shared_dot = g_own[1].astype(F32) * acc[1] + g_own[2].astype(F32) * acc[2]
    query_dot = g_own[0].astype(F32) * acc[0]
    diagonal = row == col
    for side, total in ((0, jnp.where(is_dec, query_dot, query_dot + shared_dot)), (1, shared_dot)):
        column = jnp.sum(total, axis=1, keepdims=True) * (1.0 / (N_TP * WIDE)) * inv[side] * inv[side]
        across = jnp.sum(jnp.where(diagonal, column, 0.0), axis=0, keepdims=True)
        dots[:, side * 128 : (side + 1) * 128] = jnp.broadcast_to(across, (8, 128))

    def back(i):
        grad_q = dot_nt(g_own[0], wf[0, i])
        grad_s = dot_nt(g_own[1], wf[1, i]) + dot_nt(g_own[2], wf[2, i])
        part[0, i] = jnp.where(is_dec, grad_q, grad_q + grad_s).astype(BF16)
        part[1, i] = grad_s.astype(BF16)

    def chain_at(way_hops, direction, k):
        ahead = way_hops + 1 - k
        return lax.rem(z + ahead, N_TP) if direction == 0 else lax.rem(z - ahead + N_TP, N_TP)

    def chain(side, way, k, first):
        direction, chunk = way
        rows = pl.ds(chunk * HALF, HALF)
        begin = (
            part.at[side, chain_at(hops(way), direction, k), rows] if first else rs.at[side, direction, k - 2, rows]
        )
        return remote(
            begin, rs.at[side, direction, k - 1, rows],
            rs_s.at[side, direction, chunk, k - 1], rs_r.at[side, direction, chunk, k - 1], around[direction],
        )

    def chain_dots(direction, k, first):
        begin = dots if first else rsd.at[direction, k - 2]
        return remote(begin, rsd.at[direction, k - 1], d_s.at[direction, k - 1], d_r.at[direction, k - 1], around[direction])

    half = N_TP // 2
    back(lax.rem(z + half, N_TP))
    back(lax.rem(z + half - 1, N_TP))
    back(lax.rem(z + half + 1, N_TP))

    def chain_first(side):
        for way in WAYS:
            chain(side, way, 1, True).start()

    @pl.when(is_dec)
    def _():
        chain_first(1)

    chain_first(0)
    chain_dots(0, 1, True).start()
    chain_dots(1, 1, True).start()

    def g_far():
        return remote(g_own, g_all.at[:, d], ex_s.at[2, 0], ex_r.at[2, 0], {"dp": far})

    def g_mate():
        return remote(g_own, g_all.at[:, d], ex_s.at[2, 2], ex_r.at[2, 2], {"dp": mate})

    def g_relay():
        return remote(g_all.at[:, far], g_all.at[:, far], ex_s.at[2, 3], ex_r.at[2, 3], {"dp": mate})

    g_keep = pltpu.make_async_copy(g_own, g_all.at[:, d], loc.at[6])
    g_far().start()
    g_mate().start()
    g_keep.start()

    def chain_step(k, _):
        back(lax.rem(z + half - k, N_TP))

        @pl.when(k < half)
        def _():
            back(lax.rem(z + half + k, N_TP))

        def go(side):
            for way in WAYS:
                direction, chunk = way
                last = hops(way)

                def one():
                    chain(side, way, k - 1, True).wait_recv()
                    rows = pl.ds(chunk * HALF, HALF)
                    target = chain_at(last, direction, k)
                    rs[side, direction, k - 2, rows] = (
                        rs[side, direction, k - 2, rows].astype(F32) + part[side, target, rows].astype(F32)
                    ).astype(BF16)
                    chain(side, way, k, False).start()

                if last == N_TP // 2:
                    one()
                else:
                    pl.when(k < N_TP // 2)(one)

        pl.when(is_dec)(lambda: go(1))
        go(0)
        for direction in range(2):
            def one_dots():
                chain_dots(direction, k - 1, True).wait_recv()
                rsd[direction, k - 2] = rsd[direction, k - 2] + dots[...]
                chain_dots(direction, k, False).start()

            if direction == 0:
                one_dots()
            else:
                pl.when(k < N_TP // 2)(one_dots)
        return 0

    def relay(side):
        give_far_mate(side).wait_recv()
        relay_mate(side).start()

    def settled(side):
        give_far(side).wait_recv()
        give_mate(side).wait_recv()
        relay_mate(side).wait_recv()
        keep_own(side).wait()

    def weight_gradient(w, side, out):
        for j in range(4):
            left_side = x_all[side, j].reshape(N_DP * ROWS, WIDE)
            right_side = g_all[w].reshape(N_DP * ROWS, WIDE)
            out[j] = dot_tn(left_side, right_side).astype(BF16)

    lax.fori_loop(2, 6, chain_step, 0)
    g_far().wait_recv()
    g_relay().start()
    relay(0)
    lax.fori_loop(6, 8, chain_step, 0)
    pl.when(is_dec)(lambda: relay(1))
    settled(0)
    g_mate().wait_recv()
    g_relay().wait_recv()
    g_keep.wait()
    weight_gradient(0, 0, dq_o)
    lax.fori_loop(8, N_TP // 2 + 1, chain_step, 0)
    chain_dots(0, N_TP // 2, True).wait_recv()
    chain_dots(1, N_TP // 2 - 1, True).wait_recv()
    summed = rsd[0, N_TP // 2 - 1] + rsd[1, N_TP // 2 - 2] + dots[...]

    def arrived(side, chunk):
        rows = pl.ds(chunk * HALF, HALF)
        total = part[side, z, rows].astype(F32)
        for direction in range(2):
            way = (direction, chunk)
            chain(side, way, hops(way), True).wait_recv()
            total = total + rs[side, direction, hops(way) - 1, rows].astype(F32)
        return total

    def column_of(side):
        across = jnp.broadcast_to(summed[0:1, side * 128 : (side + 1) * 128], (ROWS, ROWS))
        return jnp.sum(jnp.where(diagonal, across, 0.0), axis=1, keepdims=True)

    here = pl.ds(pl.multiple_of(z * WIDE, WIDE), WIDE)

    def give_memory(i):
        return remote(h_out.at[i], h_in.at[s - FIRST_DECODER], h_s.at[i], h_r.at[0], {"section": i})

    @pl.when(is_dec)
    def _():
        gain = fgain[0:1, here]
        column = column_of(1)
        for chunk in range(2):
            rows = slice(chunk * HALF, (chunk + 1) * HALF)
            value = gain * arrived(1, chunk) - gat[1, z, rows].astype(F32) * column[rows]
            h_out[chunk * 4 : chunk * 4 + 4] = value.reshape(4, PIECE, WIDE)
        for i in range(N_SECTION):
            @pl.when(s != i)
            def _():
                give_memory(i).start()
        pltpu.make_async_copy(h_out.at[s], h_in.at[s - FIRST_DECODER], h_r.at[0]).start()

    gain_here = lgain[0:1, here]
    stream_column = column_of(0)
    for chunk in range(2):
        rows = slice(chunk * HALF, (chunk + 1) * HALF)
        value = gain_here * arrived(0, chunk) - stream[rows].astype(F32) * stream_column[rows]
        sg_o[rows] = value.astype(BF16)

    pl.when(is_dec)(lambda: settled(1))
    weight_gradient(1, src, dk_o)
    weight_gradient(2, src, dv_o)

    pltpu.make_async_copy(h_in, h_in, h_r.at[0]).wait()
    mg_o[...] = h_in[0] + h_in[1] + h_in[2] + h_in[3]

    def drain(which):
        for way in WAYS:
            def step(k, _):
                ring(which, way, k).wait_send()
                chain(which, way, k, True).wait_send()
                return 0

            lax.fori_loop(1, hops(way) + 1, step, 0)

    drain(0)
    pl.when(is_dec)(lambda: drain(1))
    for w in range(3):
        weight_far(w).wait_send()
        weight_mate(w).wait_send()
        weight_relay(w).wait_send()
    for i in range(N_SECTION - FIRST_DECODER):
        @pl.when(s != FIRST_DECODER + i)
        def _():
            mem_send(i).wait_send()

    def drain_exchange(side):
        give_far(side).wait_send()
        give_far_mate(side).wait_send()
        give_mate(side).wait_send()
        relay_mate(side).wait_send()

    drain_exchange(0)
    pl.when(is_dec)(lambda: drain_exchange(1))
    g_far().wait_send()
    g_mate().wait_send()
    g_relay().wait_send()
    for direction in range(2):
        def step(k, _):
            chain_dots(direction, k, True).wait_send()
            return 0

        lax.fori_loop(1, N_TP // 2 + 1 - direction, step, 0)

    @pl.when(is_dec)
    def _():
        for i in range(N_SECTION):
            @pl.when(s != i)
            def _():
                give_memory(i).wait_send()


def hand_out(mix, sg, mg, dq, dk, dv, mix_o, sg_o, mg_o, dq_o, dk_o, dv_o):
    mix_o[...] = mix[...]
    sg_o[...] = sg[...]
    for n in range(4):
        mg_o[n] = mg[n * 4 : n * 4 + 4].astype(BF16)
    dq_o[...] = dq[...]
    dk_o[...] = dk[...]
    dv_o[...] = dv[...]


def shards(
    stream, memory_hidden, layer_gain, final_gain, query_weight, key_weight, value_weight,
    cotangent, encoder_lengths, decoder_lengths, assignment,
):
    vmem = pl.BlockSpec(memory_space=pltpu.VMEM)
    hbm = pl.BlockSpec(memory_space=pl.ANY)
    smem = pl.BlockSpec(memory_space=pltpu.SMEM)
    dma = pltpu.SemaphoreType.DMA
    outs = pl.pallas_call(
        body,
        name="relay",
        out_shape=(
            jax.ShapeDtypeStruct((ROWS, WIDE), BF16),
            jax.ShapeDtypeStruct((ROWS, WIDE), BF16),
            jax.ShapeDtypeStruct((PIECE, WIDE), F32),
            jax.ShapeDtypeStruct((4, WIDE, WIDE), BF16),
            jax.ShapeDtypeStruct((4, WIDE, WIDE), BF16),
            jax.ShapeDtypeStruct((4, WIDE, WIDE), BF16),
        ),
        in_specs=[vmem, vmem, vmem, vmem, hbm, hbm, hbm, vmem, smem, smem, smem],
        out_specs=(vmem,) * 6,
        scratch_shapes=[
            pltpu.VMEM((PIECE, WIDE), BF16),
            pltpu.VMEM((2, N_TP, ROWS, WIDE), BF16),
            pltpu.VMEM((2, N_TP, ROWS, WIDE), BF16),
            pltpu.VMEM((3, N_TP, WIDE, WIDE), BF16),
            pltpu.VMEM((3, ROWS, WIDE), F32),
            pltpu.VMEM((2, ROWS, 128), F32),
            pltpu.VMEM((3, ROWS, WIDE), BF16),
            pltpu.VMEM((3, N_DP, ROWS, WIDE), BF16),
            pltpu.VMEM((2, 4, N_DP, ROWS, WIDE), BF16),
            pltpu.VMEM((2, 4, ROWS, WIDE), BF16),
            pltpu.VMEM((2, N_TP, ROWS, WIDE), BF16),
            pltpu.VMEM((2, 2, N_TP // 2, ROWS, WIDE), BF16),
            pltpu.VMEM((8, 256), F32),
            pltpu.VMEM((2, N_TP // 2, 8, 256), F32),
            pltpu.VMEM((N_SECTION, PIECE, WIDE), F32),
            pltpu.VMEM((N_SECTION - FIRST_DECODER, PIECE, WIDE), F32),
            dma((2, 2, 2, 8)), dma((2, 2, 2, 8)),
            dma((3,)), dma((3,)), dma((3,)), dma((3,)), dma((3,)), dma((3,)),
            dma((4,)), dma((1,)),
            dma((3, 4)), dma((3, 4)),
            dma((2, 2, 2, 8)), dma((2, 2, 2, 8)),
            dma((2, 8)), dma((2, 8)),
            dma((8,)), dma((1,)),
            dma((7,)),
        ],
        compiler_params=pltpu.CompilerParams(
            collective_id=0, has_side_effects=True, vmem_limit_bytes=60 * 1024 * 1024
        ),
    )(
        stream.reshape(ROWS, WIDE),
        memory_hidden,
        layer_gain,
        final_gain.reshape(1, N_TP * WIDE),
        query_weight.reshape(4, WIDE, WIDE),
        key_weight.reshape(4, WIDE, WIDE),
        value_weight.reshape(4, WIDE, WIDE),
        cotangent.reshape(ROWS, WIDE),
        encoder_lengths,
        decoder_lengths,
        assignment.reshape(4),
    )
    mixture, stream_grad, memory_grad, dq, dk, dv = pl.pallas_call(
        hand_out,
        name="hand_out",
        out_shape=(
            jax.ShapeDtypeStruct((ROWS, WIDE), BF16),
            jax.ShapeDtypeStruct((ROWS, WIDE), BF16),
            jax.ShapeDtypeStruct((4, 4, WIDE), BF16),
            jax.ShapeDtypeStruct((4, WIDE, WIDE), BF16),
            jax.ShapeDtypeStruct((4, WIDE, WIDE), BF16),
            jax.ShapeDtypeStruct((4, WIDE, WIDE), BF16),
        ),
        in_specs=[vmem] * 6,
        out_specs=(vmem,) * 6,
    )(*outs)
    rows = (1, 4, 32, WIDE)
    square = (1, 4 * WIDE, WIDE)
    return (
        mixture.reshape(rows),
        stream_grad.reshape(rows),
        memory_grad,
        dq.reshape(square),
        dk.reshape(square),
        dv.reshape(square),
    )


def solution(mesh):
    tokens = P("section", "dp", None, "tp")
    weight = P("section", "dp", "tp")
    memory = P("dp", "section", "tp")
    return jax.shard_map(
        shards,
        mesh=mesh,
        in_specs=(
            tokens, memory, P("section", None), P(), weight, weight, weight, tokens, P("dp"), P("dp"), P("dp", None),
        ),
        out_specs=(tokens, tokens, memory, weight, weight, weight),
        check_vma=False,
    )
```

```python
import functools

import jax
import jax.numpy as jnp
from jax import lax
from jax.experimental import pallas as pl
from jax.experimental.pallas import tpu as pltpu
from jax.sharding import PartitionSpec as P

MESH = pl.DeviceIdType.MESH
F32 = jnp.float32
BF16 = jnp.bfloat16
EPSILON = 1e-06
HEAD_DIM = 64
N_SECTION = 8
N_TP = 16
N_DP = 4
ROWS = 128
WIDE = 256
HALF = 64
PIECE = 16
FIRST_DECODER = N_SECTION // 2
WAYS = [(0, 0), (1, 0), (0, 1), (1, 1)]


def dot_nn(a, b):
    return lax.dot_general(a, b, (((1,), (0,)), ((), ())), preferred_element_type=F32)


def dot_nt(a, b):
    return lax.dot_general(a, b, (((1,), (1,)), ((), ())), preferred_element_type=F32)


def dot_tn(a, b):
    return lax.dot_general(a, b, (((0,), (0,)), ((), ())), preferred_element_type=F32)


def hops(way):
    return N_TP // 2 if way[0] == way[1] else N_TP // 2 - 1


def body(
    stream, mem, lgain, fgain, wq, wk, wv, cot, enc_len, dec_len, assign,
    mix_o, sg_o, mg_o, dq_o, dk_o, dv_o,
    piece, gat, xm, sq, wf, acc, inv, g_own, g_all, x_all, x_rel, part, rs, dots, rsd, h_out, h_in,
    ag_s, ag_r, wy_s, wy_r, wc_s, wc_r, wr_s, wr_r, m_s, m_r, ex_s, ex_r, rs_s, rs_r, d_s, d_r, h_s, h_r, loc,
):
    s = lax.axis_index("section")
    z = lax.axis_index("tp")
    d = lax.axis_index("dp")
    is_dec = s >= FIRST_DECODER
    src = jnp.where(is_dec, 1, 0)
    core = lax.rem(d, 2)
    chip = lax.div(d, 2)
    mate = d + 1 - 2 * core
    far = lax.rem(d + 2, N_DP)
    far_mate = lax.rem(mate + 2, N_DP)
    right = {"tp": lax.rem(z + 1, N_TP)}
    left = {"tp": lax.rem(z + N_TP - 1, N_TP)}
    around = [right, left]

    def remote(a, b, ss, rr, to):
        return pltpu.make_async_remote_copy(
            src_ref=a, dst_ref=b, send_sem=ss, recv_sem=rr, device_id=to, device_id_type=MESH
        )

    barrier = pltpu.get_barrier_semaphore()
    for to in (right, left, {"dp": mate}, {"dp": far}):
        pl.semaphore_signal(barrier, inc=1, device_id=to, device_id_type=MESH)
    for other in range(1, N_SECTION):
        pl.semaphore_signal(
            barrier, inc=1, device_id={"section": lax.rem(s + other, N_SECTION)}, device_id_type=MESH
        )

    own = [
        pltpu.make_async_copy(stream, gat.at[0, z], loc.at[0]),
        pltpu.make_async_copy(wq, wf.at[0, pl.ds(4 * d, 4)], loc.at[1]),
        pltpu.make_async_copy(wk, wf.at[1, pl.ds(4 * d, 4)], loc.at[2]),
        pltpu.make_async_copy(wv, wf.at[2, pl.ds(4 * d, 4)], loc.at[3]),
    ]
    for c in own[1:]:
        c.start()
    own[0].start()
    piece[...] = jnp.concatenate([mem[n].astype(F32) for n in range(4)], axis=0).astype(BF16)
    for side in range(2):
        sq[side] = jnp.zeros((ROWS, WIDE), F32)
    for w in range(3):
        acc[w] = jnp.zeros((ROWS, WIDE), F32)
    pl.semaphore_wait(barrier, N_SECTION + 3)

    def ring(which, way, k):
        direction, chunk = way
        rows = pl.ds(chunk * HALF, HALF)
        back = k - 1 if direction == 0 else 1 - k
        at = lax.rem(z - back + N_TP, N_TP)
        return remote(
            gat.at[which, at, rows], gat.at[which, at, rows],
            ag_s.at[which, direction, chunk, k - 1], ag_r.at[which, direction, chunk, k - 1],
            around[direction],
        )

    def weight_far(w):
        return remote(
            wf.at[w, pl.ds(4 * d, 4)], wf.at[w, pl.ds(4 * d, 4)], wy_s.at[w], wy_r.at[w], {"dp": far}
        )

    def weight_mate(w):
        return remote(
            wf.at[w, pl.ds(4 * d, 4)], wf.at[w, pl.ds(4 * d, 4)], wc_s.at[w], wc_r.at[w], {"dp": mate}
        )

    def weight_relay(w):
        return remote(
            wf.at[w, pl.ds(4 * far, 4)], wf.at[w, pl.ds(4 * far, 4)], wr_s.at[w], wr_r.at[w], {"dp": mate}
        )

    def mem_send(i):
        return remote(
            piece, gat.at[1, z, pl.ds(s * PIECE, PIECE)], m_s.at[i], m_r.at[0], {"section": FIRST_DECODER + i}
        )

    def mem_keep():
        return pltpu.make_async_copy(piece, gat.at[1, z, pl.ds(s * PIECE, PIECE)], m_r.at[0])

    for i in range(N_SECTION - FIRST_DECODER):
        @pl.when(s != FIRST_DECODER + i)
        def _():
            mem_send(i).start()

    @pl.when(is_dec)
    def _():
        mem_keep().start()

    own[0].wait()
    for way in WAYS:
        ring(0, way, 1).start()
    for w in range(3):
        own[1 + w].wait()
        weight_far(w).start()

    for w in range(3):
        weight_mate(w).start()

    @pl.when(is_dec)
    def _():
        pltpu.make_async_copy(gat.at[1, z], gat.at[1, z], m_r.at[0]).wait()
        for way in WAYS:
            ring(1, way, 1).start()

    half = N_TP // 2

    def take(side, i):
        value = gat[side, i].astype(F32)
        gain = (lgain, fgain)[side][0:1, pl.ds(pl.multiple_of(i * WIDE, WIDE), WIDE)]
        xm[side, i] = (value * gain).astype(BF16)
        sq[side] = sq[side] + value * value

    def near(side, i):
        def add(w):
            acc[w] = acc[w] + dot_nn(xm[side, i], wf[w, i])

        @pl.when(lax.div(i, half) == chip)
        def _():
            if side == 0:
                add(0)

                @pl.when(jnp.logical_not(is_dec))
                def _():
                    add(1)
                    add(2)
            else:
                add(1)
                add(2)

    def both_sides(f, i):
        f(0, i)
        pl.when(is_dec)(lambda: f(1, i))

    def ring_step(k, multiply):
        for which in range(2):
            def go():
                for way in WAYS:
                    ring(which, way, k - 1).wait_recv()
                    if hops(way) == half:
                        ring(which, way, k).start()
                    else:
                        @pl.when(k < half)
                        def _():
                            ring(which, way, k).start()
            if which == 0:
                go()
            else:
                pl.when(is_dec)(go)
        for i in (lax.rem(z + N_TP + 1 - k, N_TP), lax.rem(z + k - 1, N_TP)):
            both_sides(take, i)
            if multiply:
                both_sides(near, i)

    def early(k, carry):
        ring_step(k, False)
        return carry

    def later(k, carry):
        ring_step(k, True)
        return carry

    both_sides(take, z)
    lax.fori_loop(2, 4, early, 0)
    for w in range(3):
        weight_mate(w).wait_recv()
    for distance in (0, 1, -1, 2, -2):
        both_sides(near, lax.rem(z + distance + N_TP, N_TP))
    lax.fori_loop(4, 6, later, 0)
    weight_far(0).wait_recv()
    weight_relay(0).start()
    lax.fori_loop(6, half + 1, later, 0)

    def ring_end(side):
        for way in WAYS:
            if hops(way) == half:
                ring(side, way, half).wait_recv()
        opposite = lax.rem(z + half, N_TP)
        take(side, opposite)
        near(side, opposite)

    ring_end(0)
    pl.when(is_dec)(lambda: ring_end(1))
    weight_far(1).wait_recv()
    weight_relay(1).start()

    def row_scale(side):
        mean = jnp.sum(sq[side], axis=1, keepdims=True) * (1.0 / (N_TP * WIDE))
        return jnp.broadcast_to(lax.rsqrt(mean + EPSILON), (ROWS, 128))

    stream_inverse = row_scale(0)
    inv[0] = stream_inverse
    inv[1] = stream_inverse

    @pl.when(is_dec)
    def _():
        inv[1] = row_scale(1)

    def give_far(side):
        return remote(
            xm.at[side, pl.ds(4 * far, 4)], x_all.at[side, :, d], ex_s.at[side, 0], ex_r.at[side, 0], {"dp": far}
        )

    def give_far_mate(side):
        return remote(
            xm.at[side, pl.ds(4 * far_mate, 4)], x_rel.at[side], ex_s.at[side, 1], ex_r.at[side, 1], {"dp": far}
        )

    def give_mate(side):
        return remote(
            xm.at[side, pl.ds(4 * mate, 4)], x_all.at[side, :, d], ex_s.at[side, 2], ex_r.at[side, 2], {"dp": mate}
        )

    def relay_mate(side):
        return remote(
            x_rel.at[side], x_all.at[side, :, far], ex_s.at[side, 3], ex_r.at[side, 3], {"dp": mate}
        )

    def keep_own(side):
        return pltpu.make_async_copy(xm.at[side, pl.ds(4 * d, 4)], x_all.at[side, :, d], loc.at[4 + side])

    def start_exchange(side):
        give_far_mate(side).start()
        give_far(side).start()
        give_mate(side).start()
        keep_own(side).start()

    start_exchange(0)

    def project(w):
        side = 0 if w == 0 else src
        begin = (1 - chip) * half

        def step(i, total):
            return total + dot_nn(xm[side, begin + i], wf[w, begin + i])

        acc[w] = lax.fori_loop(0, half, step, acc[w])

    for w in range(3):
        if w == 2:
            weight_far(2).wait_recv()
            weight_relay(2).start()
        weight_relay(w).wait_recv()
        project(w)

    row = lax.broadcasted_iota(jnp.int32, (ROWS, ROWS), 0)
    col = lax.broadcasted_iota(jnp.int32, (ROWS, ROWS), 1)
    row_sample = lax.shift_right_logical(row, 5)
    col_sample = jnp.where(
        is_dec, jnp.bitwise_and(lax.shift_right_logical(col, 2), 3), lax.shift_right_logical(col, 5)
    )
    col_slot = jnp.where(
        is_dec, lax.shift_right_logical(col, 4) * 4 + jnp.bitwise_and(col, 3), jnp.bitwise_and(col, 31)
    )
    wanted = jnp.zeros((ROWS, ROWS), jnp.int32)
    key_len = jnp.zeros((ROWS, ROWS), jnp.int32)
    query_len = jnp.zeros((ROWS, ROWS), jnp.int32)
    for m in range(4):
        chosen = jnp.where(is_dec, assign[m], m)
        length = jnp.where(is_dec, dec_len[m], enc_len[m])
        wanted = jnp.where(row_sample == m, chosen, wanted)
        key_len = jnp.where(col_sample == m, enc_len[m], key_len)
        query_len = jnp.where(row_sample == m, length, query_len)
    live = jnp.logical_and(wanted == col_sample, col_slot < key_len)
    row_live = (jnp.bitwise_and(row, 31) < query_len).astype(F32)[:, 0:HEAD_DIM]

    q_scale = jnp.concatenate([inv[0], inv[0]], axis=1)
    s_scale = jnp.concatenate([inv[1], inv[1]], axis=1)
    queries = (acc[0] * q_scale).astype(BF16)
    keys = (acc[1] * s_scale).astype(BF16)
    values = (acc[2] * s_scale).astype(BF16)
    scale = HEAD_DIM**-0.5
    for h in range(WIDE // HEAD_DIM):
        at = slice(h * HEAD_DIM, (h + 1) * HEAD_DIM)
        qh, kh, vh = queries[:, at], keys[:, at], values[:, at]
        scores = jnp.where(live, dot_nt(qh, kh) * scale, -1e30)
        raised = jnp.exp(scores - jnp.max(scores, axis=1, keepdims=True))
        weights = raised / jnp.sum(raised, axis=1, keepdims=True)
        probs = weights.astype(BF16)
        mix_o[:, at] = (dot_nn(probs, vh) * row_live).astype(BF16)
        upstream = (cot[:, at].astype(F32) * row_live).astype(BF16)
        grad_weights = dot_nt(upstream, vh)
        inner = jnp.sum(grad_weights * weights, axis=1, keepdims=True)
        grad_scores = (weights * (grad_weights - inner) * scale).astype(BF16)
        g_own[0, :, at] = (dot_nn(grad_scores, kh) * inv[0][:, 0:HEAD_DIM]).astype(BF16)
        g_own[1, :, at] = (dot_tn(grad_scores, qh) * inv[1][:, 0:HEAD_DIM]).astype(BF16)
        g_own[2, :, at] = (dot_tn(probs, upstream) * inv[1][:, 0:HEAD_DIM]).astype(BF16)

    shared_dot = g_own[1].astype(F32) * acc[1] + g_own[2].astype(F32) * acc[2]
    query_dot = g_own[0].astype(F32) * acc[0]
    diagonal = row == col
    for side, total in ((0, jnp.where(is_dec, query_dot, query_dot + shared_dot)), (1, shared_dot)):
        column = jnp.sum(total, axis=1, keepdims=True) * (1.0 / (N_TP * WIDE)) * inv[side] * inv[side]
        across = jnp.sum(jnp.where(diagonal, column, 0.0), axis=0, keepdims=True)
        dots[:, side * 128 : (side + 1) * 128] = jnp.broadcast_to(across, (8, 128))

    def back(i):
        grad_q = dot_nt(g_own[0], wf[0, i])
        grad_s = dot_nt(g_own[1], wf[1, i]) + dot_nt(g_own[2], wf[2, i])
        part[0, i] = jnp.where(is_dec, grad_q, grad_q + grad_s).astype(BF16)
        part[1, i] = grad_s.astype(BF16)

    def chain_at(way_hops, direction, k):
        ahead = way_hops + 1 - k
        return lax.rem(z + ahead, N_TP) if direction == 0 else lax.rem(z - ahead + N_TP, N_TP)

    def chain(side, way, k, first):
        direction, chunk = way
        rows = pl.ds(chunk * HALF, HALF)
        begin = (
            part.at[side, chain_at(hops(way), direction, k), rows] if first else rs.at[side, direction, k - 2, rows]
        )
        return remote(
            begin, rs.at[side, direction, k - 1, rows],
            rs_s.at[side, direction, chunk, k - 1], rs_r.at[side, direction, chunk, k - 1], around[direction],
        )

    def chain_dots(direction, k, first):
        begin = dots if first else rsd.at[direction, k - 2]
        return remote(begin, rsd.at[direction, k - 1], d_s.at[direction, k - 1], d_r.at[direction, k - 1], around[direction])

    back(lax.rem(z + half, N_TP))
    back(lax.rem(z + half - 1, N_TP))
    back(lax.rem(z + half + 1, N_TP))

    def chain_first(side):
        for way in WAYS:
            chain(side, way, 1, True).start()

    @pl.when(is_dec)
    def _():
        chain_first(1)

    chain_first(0)
    chain_dots(0, 1, True).start()
    chain_dots(1, 1, True).start()

    def g_far():
        return remote(g_own, g_all.at[:, d], ex_s.at[2, 0], ex_r.at[2, 0], {"dp": far})

    def g_mate():
        return remote(g_own, g_all.at[:, d], ex_s.at[2, 2], ex_r.at[2, 2], {"dp": mate})

    def g_relay():
        return remote(g_all.at[:, far], g_all.at[:, far], ex_s.at[2, 3], ex_r.at[2, 3], {"dp": mate})

    g_keep = pltpu.make_async_copy(g_own, g_all.at[:, d], loc.at[6])
    g_far().start()
    g_mate().start()
    g_keep.start()
    pl.when(is_dec)(lambda: start_exchange(1))

    def chain_step(k, _):
        back(lax.rem(z + half - k, N_TP))

        @pl.when(k < half)
        def _():
            back(lax.rem(z + half + k, N_TP))

        def go(side):
            for way in WAYS:
                direction, chunk = way
                last = hops(way)

                def one():
                    chain(side, way, k - 1, True).wait_recv()
                    rows = pl.ds(chunk * HALF, HALF)
                    target = chain_at(last, direction, k)
                    rs[side, direction, k - 2, rows] = (
                        rs[side, direction, k - 2, rows].astype(F32) + part[side, target, rows].astype(F32)
                    ).astype(BF16)
                    chain(side, way, k, False).start()

                if last == N_TP // 2:
                    one()
                else:
                    pl.when(k < N_TP // 2)(one)

        pl.when(is_dec)(lambda: go(1))
        go(0)
        for direction in range(2):
            def one_dots():
                chain_dots(direction, k - 1, True).wait_recv()
                rsd[direction, k - 2] = rsd[direction, k - 2] + dots[...]
                chain_dots(direction, k, False).start()

            if direction == 0:
                one_dots()
            else:
                pl.when(k < N_TP // 2)(one_dots)
        return 0

    def relay(side):
        give_far_mate(side).wait_recv()
        relay_mate(side).start()

    def settled(side):
        give_far(side).wait_recv()
        give_mate(side).wait_recv()
        relay_mate(side).wait_recv()
        keep_own(side).wait()

    def weight_gradient(w, side, out):
        for j in range(4):
            left_side = x_all[side, j].reshape(N_DP * ROWS, WIDE)
            right_side = g_all[w].reshape(N_DP * ROWS, WIDE)
            out[j] = dot_tn(left_side, right_side).astype(BF16)

    lax.fori_loop(2, 6, chain_step, 0)
    g_far().wait_recv()
    g_relay().start()
    relay(0)
    lax.fori_loop(6, 8, chain_step, 0)
    settled(0)
    g_mate().wait_recv()
    g_relay().wait_recv()
    g_keep.wait()
    weight_gradient(0, 0, dq_o)
    lax.fori_loop(8, N_TP // 2 + 1, chain_step, 0)
    chain_dots(0, N_TP // 2, True).wait_recv()
    chain_dots(1, N_TP // 2 - 1, True).wait_recv()
    summed = rsd[0, N_TP // 2 - 1] + rsd[1, N_TP // 2 - 2] + dots[...]

    def arrived(side, chunk):
        rows = pl.ds(chunk * HALF, HALF)
        total = part[side, z, rows].astype(F32)
        for direction in range(2):
            way = (direction, chunk)
            chain(side, way, hops(way), True).wait_recv()
            total = total + rs[side, direction, hops(way) - 1, rows].astype(F32)
        return total

    def column_of(side):
        across = jnp.broadcast_to(summed[0:1, side * 128 : (side + 1) * 128], (ROWS, ROWS))
        return jnp.sum(jnp.where(diagonal, across, 0.0), axis=1, keepdims=True)

    here = pl.ds(pl.multiple_of(z * WIDE, WIDE), WIDE)

    def give_memory(i):
        return remote(h_out.at[i], h_in.at[s - FIRST_DECODER], h_s.at[i], h_r.at[0], {"section": i})

    @pl.when(is_dec)
    def _():
        gain = fgain[0:1, here]
        column = column_of(1)
        for chunk in range(2):
            rows = slice(chunk * HALF, (chunk + 1) * HALF)
            value = gain * arrived(1, chunk) - gat[1, z, rows].astype(F32) * column[rows]
            h_out[chunk * 4 : chunk * 4 + 4] = value.reshape(4, PIECE, WIDE)
        for i in range(N_SECTION):
            @pl.when(s != i)
            def _():
                give_memory(i).start()
        pltpu.make_async_copy(h_out.at[s], h_in.at[s - FIRST_DECODER], h_r.at[0]).start()

    gain_here = lgain[0:1, here]
    stream_column = column_of(0)
    for chunk in range(2):
        rows = slice(chunk * HALF, (chunk + 1) * HALF)
        value = gain_here * arrived(0, chunk) - stream[rows].astype(F32) * stream_column[rows]
        sg_o[rows] = value.astype(BF16)

    pl.when(is_dec)(lambda: relay(1))
    pl.when(is_dec)(lambda: settled(1))
    weight_gradient(1, src, dk_o)
    weight_gradient(2, src, dv_o)

    pltpu.make_async_copy(h_in, h_in, h_r.at[0]).wait()
    mg_o[...] = h_in[0] + h_in[1] + h_in[2] + h_in[3]

    def drain(which):
        for way in WAYS:
            def step(k, _):
                ring(which, way, k).wait_send()
                chain(which, way, k, True).wait_send()
                return 0

            lax.fori_loop(1, hops(way) + 1, step, 0)

    drain(0)
    pl.when(is_dec)(lambda: drain(1))
    for w in range(3):
        weight_far(w).wait_send()
        weight_mate(w).wait_send()
        weight_relay(w).wait_send()
    for i in range(N_SECTION - FIRST_DECODER):
        @pl.when(s != FIRST_DECODER + i)
        def _():
            mem_send(i).wait_send()

    def drain_exchange(side):
        give_far(side).wait_send()
        give_far_mate(side).wait_send()
        give_mate(side).wait_send()
        relay_mate(side).wait_send()

    drain_exchange(0)
    pl.when(is_dec)(lambda: drain_exchange(1))
    g_far().wait_send()
    g_mate().wait_send()
    g_relay().wait_send()
    for direction in range(2):
        def step(k, _):
            chain_dots(direction, k, True).wait_send()
            return 0

        lax.fori_loop(1, N_TP // 2 + 1 - direction, step, 0)

    @pl.when(is_dec)
    def _():
        for i in range(N_SECTION):
            @pl.when(s != i)
            def _():
                give_memory(i).wait_send()


def hand_out(mg, mix, sg, dq, dk, dv, mg_o, mix_o, sg_o, dq_o, dk_o, dv_o, small, large, sem):
    places = (small.at[0], small.at[1], large.at[0], large.at[1], large.at[2])
    taken = [
        pltpu.make_async_copy(a, b, sem.at[0, n]) for n, (a, b) in enumerate(zip((mix, sg, dq, dk, dv), places))
    ]
    given = [
        pltpu.make_async_copy(a, b, sem.at[1, n])
        for n, (a, b) in enumerate(zip(places, (mix_o, sg_o, dq_o, dk_o, dv_o)))
    ]
    for c in taken:
        c.start()
    for n in range(4):
        mg_o[n] = mg[n * 4 : n * 4 + 4].astype(BF16)
    for a, b in zip(taken, given):
        a.wait()
        b.start()
    for c in given:
        c.wait()


def shards(
    stream, memory_hidden, layer_gain, final_gain, query_weight, key_weight, value_weight,
    cotangent, encoder_lengths, decoder_lengths, assignment,
):
    vmem = pl.BlockSpec(memory_space=pltpu.VMEM)
    hbm = pl.BlockSpec(memory_space=pl.ANY)
    smem = pl.BlockSpec(memory_space=pltpu.SMEM)
    dma = pltpu.SemaphoreType.DMA
    outs = pl.pallas_call(
        body,
        name="relay",
        out_shape=(
            jax.ShapeDtypeStruct((ROWS, WIDE), BF16),
            jax.ShapeDtypeStruct((ROWS, WIDE), BF16),
            jax.ShapeDtypeStruct((PIECE, WIDE), F32),
            jax.ShapeDtypeStruct((4, WIDE, WIDE), BF16),
            jax.ShapeDtypeStruct((4, WIDE, WIDE), BF16),
            jax.ShapeDtypeStruct((4, WIDE, WIDE), BF16),
        ),
        in_specs=[vmem, vmem, vmem, vmem, hbm, hbm, hbm, vmem, smem, smem, smem],
        out_specs=(vmem,) * 6,
        scratch_shapes=[
            pltpu.VMEM((PIECE, WIDE), BF16),
            pltpu.VMEM((2, N_TP, ROWS, WIDE), BF16),
            pltpu.VMEM((2, N_TP, ROWS, WIDE), BF16),
            pltpu.VMEM((2, ROWS, WIDE), F32),
            pltpu.VMEM((3, N_TP, WIDE, WIDE), BF16),
            pltpu.VMEM((3, ROWS, WIDE), F32),
            pltpu.VMEM((2, ROWS, 128), F32),
            pltpu.VMEM((3, ROWS, WIDE), BF16),
            pltpu.VMEM((3, N_DP, ROWS, WIDE), BF16),
            pltpu.VMEM((2, 4, N_DP, ROWS, WIDE), BF16),
            pltpu.VMEM((2, 4, ROWS, WIDE), BF16),
            pltpu.VMEM((2, N_TP, ROWS, WIDE), BF16),
            pltpu.VMEM((2, 2, N_TP // 2, ROWS, WIDE), BF16),
            pltpu.VMEM((8, 256), F32),
            pltpu.VMEM((2, N_TP // 2, 8, 256), F32),
            pltpu.VMEM((N_SECTION, PIECE, WIDE), F32),
            pltpu.VMEM((N_SECTION - FIRST_DECODER, PIECE, WIDE), F32),
            dma((2, 2, 2, 8)), dma((2, 2, 2, 8)),
            dma((3,)), dma((3,)), dma((3,)), dma((3,)), dma((3,)), dma((3,)),
            dma((4,)), dma((1,)),
            dma((3, 4)), dma((3, 4)),
            dma((2, 2, 2, 8)), dma((2, 2, 2, 8)),
            dma((2, 8)), dma((2, 8)),
            dma((8,)), dma((1,)),
            dma((7,)),
        ],
        compiler_params=pltpu.CompilerParams(
            collective_id=0, has_side_effects=True, vmem_limit_bytes=60 * 1024 * 1024
        ),
    )(
        stream.reshape(ROWS, WIDE),
        memory_hidden,
        layer_gain,
        final_gain.reshape(1, N_TP * WIDE),
        query_weight.reshape(4, WIDE, WIDE),
        key_weight.reshape(4, WIDE, WIDE),
        value_weight.reshape(4, WIDE, WIDE),
        cotangent.reshape(ROWS, WIDE),
        encoder_lengths,
        decoder_lengths,
        assignment.reshape(4),
    )
    mixture, stream_grad, memory_grad, dq, dk, dv = outs
    memory_grad, mixture, stream_grad, dq, dk, dv = pl.pallas_call(
        hand_out,
        name="hand_out",
        out_shape=(
            jax.ShapeDtypeStruct((4, 4, WIDE), BF16),
            jax.ShapeDtypeStruct((ROWS, WIDE), BF16),
            jax.ShapeDtypeStruct((ROWS, WIDE), BF16),
            jax.ShapeDtypeStruct((4, WIDE, WIDE), BF16),
            jax.ShapeDtypeStruct((4, WIDE, WIDE), BF16),
            jax.ShapeDtypeStruct((4, WIDE, WIDE), BF16),
        ),
        in_specs=[vmem] + [hbm] * 5,
        out_specs=(vmem,) + (hbm,) * 5,
        scratch_shapes=[
            pltpu.VMEM((2, ROWS, WIDE), BF16),
            pltpu.VMEM((3, 4, WIDE, WIDE), BF16),
            dma((2, 5)),
        ],
    )(memory_grad, mixture, stream_grad, dq, dk, dv)
    rows = (1, 4, 32, WIDE)
    square = (1, 4 * WIDE, WIDE)
    return (
        mixture.reshape(rows),
        stream_grad.reshape(rows),
        memory_grad,
        dq.reshape(square),
        dk.reshape(square),
        dv.reshape(square),
    )


def solution(mesh):
    tokens = P("section", "dp", None, "tp")
    weight = P("section", "dp", "tp")
    memory = P("dp", "section", "tp")
    return jax.shard_map(
        shards,
        mesh=mesh,
        in_specs=(
            tokens, memory, P("section", None), P(), weight, weight, weight, tokens, P("dp"), P("dp"), P("dp", None),
        ),
        out_specs=(tokens, tokens, memory, weight, weight, weight),
        check_vma=False,
    )
```

```python
import functools

import jax
import jax.numpy as jnp
from jax import lax
from jax.experimental import pallas as pl
from jax.experimental.pallas import tpu as pltpu
from jax.sharding import PartitionSpec as P

MESH = pl.DeviceIdType.MESH
F32 = jnp.float32
BF16 = jnp.bfloat16
EPSILON = 1e-06
HEAD_DIM = 64
N_SECTION = 8
N_TP = 16
N_DP = 4
ROWS = 128
WIDE = 256
HALF = 64
PIECE = 16
FIRST_DECODER = N_SECTION // 2
WAYS = [(0, 0), (1, 0), (0, 1), (1, 1)]


def dot_nn(a, b):
    return lax.dot_general(a, b, (((1,), (0,)), ((), ())), preferred_element_type=F32)


def dot_nt(a, b):
    return lax.dot_general(a, b, (((1,), (1,)), ((), ())), preferred_element_type=F32)


def dot_tn(a, b):
    return lax.dot_general(a, b, (((0,), (0,)), ((), ())), preferred_element_type=F32)


def hops(way):
    return N_TP // 2 if way[0] == way[1] else N_TP // 2 - 1


def body(
    stream, mem, lgain, fgain, wq, wk, wv, cot, enc_len, dec_len, assign,
    mix_o, sg_o, mg_o, dq_o, dk_o, dv_o,
    piece, gat, xm, sq, wf, acc, inv, qkv, soft, up, g_own, g_all, x_all, x_rel, part, rs, dots, rsd, h_out, h_in,
    ag_s, ag_r, wy_s, wy_r, wc_s, wc_r, wr_s, wr_r, m_s, m_r, ex_s, ex_r, rs_s, rs_r, d_s, d_r, h_s, h_r, loc,
):
    s = lax.axis_index("section")
    z = lax.axis_index("tp")
    d = lax.axis_index("dp")
    is_dec = s >= FIRST_DECODER
    src = jnp.where(is_dec, 1, 0)
    core = lax.rem(d, 2)
    chip = lax.div(d, 2)
    mate = d + 1 - 2 * core
    far = lax.rem(d + 2, N_DP)
    far_mate = lax.rem(mate + 2, N_DP)
    right = {"tp": lax.rem(z + 1, N_TP)}
    left = {"tp": lax.rem(z + N_TP - 1, N_TP)}
    around = [right, left]

    def remote(a, b, ss, rr, to):
        return pltpu.make_async_remote_copy(
            src_ref=a, dst_ref=b, send_sem=ss, recv_sem=rr, device_id=to, device_id_type=MESH
        )

    barrier = pltpu.get_barrier_semaphore()
    for to in (right, left, {"dp": mate}, {"dp": far}):
        pl.semaphore_signal(barrier, inc=1, device_id=to, device_id_type=MESH)
    for other in range(1, N_SECTION):
        pl.semaphore_signal(
            barrier, inc=1, device_id={"section": lax.rem(s + other, N_SECTION)}, device_id_type=MESH
        )

    own = [
        pltpu.make_async_copy(stream, gat.at[0, z], loc.at[0]),
        pltpu.make_async_copy(wq, wf.at[0, pl.ds(4 * d, 4)], loc.at[1]),
        pltpu.make_async_copy(wk, wf.at[1, pl.ds(4 * d, 4)], loc.at[2]),
        pltpu.make_async_copy(wv, wf.at[2, pl.ds(4 * d, 4)], loc.at[3]),
    ]
    for c in own[1:]:
        c.start()
    own[0].start()
    piece[...] = jnp.concatenate([mem[n].astype(F32) for n in range(4)], axis=0).astype(BF16)
    for side in range(2):
        sq[side] = jnp.zeros((ROWS, WIDE), F32)
    for w in range(3):
        acc[w] = jnp.zeros((ROWS, WIDE), F32)
    pl.semaphore_wait(barrier, N_SECTION + 3)

    def ring(which, way, k):
        direction, chunk = way
        rows = pl.ds(chunk * HALF, HALF)
        back = k - 1 if direction == 0 else 1 - k
        at = lax.rem(z - back + N_TP, N_TP)
        return remote(
            gat.at[which, at, rows], gat.at[which, at, rows],
            ag_s.at[which, direction, chunk, k - 1], ag_r.at[which, direction, chunk, k - 1],
            around[direction],
        )

    def weight_part(w, quarter, owner):
        if w < 2:
            return wf.at[w, pl.ds(4 * owner, 4)], w
        return wf.at[w, pl.ds(4 * owner + quarter, 1)], w + quarter

    def weight_far(w, quarter=0):
        block, at = weight_part(w, quarter, d)
        return remote(block, block, wy_s.at[at], wy_r.at[at], {"dp": far})

    def weight_mate(w):
        return remote(
            wf.at[w, pl.ds(4 * d, 4)], wf.at[w, pl.ds(4 * d, 4)], wc_s.at[w], wc_r.at[w], {"dp": mate}
        )

    def weight_relay(w, quarter=0):
        block, at = weight_part(w, quarter, far)
        return remote(block, block, wr_s.at[at], wr_r.at[at], {"dp": mate})

    def mem_send(i):
        return remote(
            piece, gat.at[1, z, pl.ds(s * PIECE, PIECE)], m_s.at[i], m_r.at[0], {"section": FIRST_DECODER + i}
        )

    def mem_keep():
        return pltpu.make_async_copy(piece, gat.at[1, z, pl.ds(s * PIECE, PIECE)], m_r.at[0])

    for i in range(N_SECTION - FIRST_DECODER):
        @pl.when(s != FIRST_DECODER + i)
        def _():
            mem_send(i).start()

    @pl.when(is_dec)
    def _():
        mem_keep().start()

    own[0].wait()
    for way in WAYS:
        ring(0, way, 1).start()
    for w in range(3):
        own[1 + w].wait()
        for quarter in range(4 if w == 2 else 1):
            weight_far(w, quarter).start()

    for w in range(3):
        weight_mate(w).start()

    @pl.when(is_dec)
    def _():
        pltpu.make_async_copy(gat.at[1, z], gat.at[1, z], m_r.at[0]).wait()
        for way in WAYS:
            ring(1, way, 1).start()

    half = N_TP // 2

    def take(side, i):
        value = gat[side, i].astype(F32)
        gain = (lgain, fgain)[side][0:1, pl.ds(pl.multiple_of(i * WIDE, WIDE), WIDE)]
        xm[side, i] = (value * gain).astype(BF16)
        sq[side] = sq[side] + value * value

    def near(side, i):
        def add(w):
            acc[w] = acc[w] + dot_nn(xm[side, i], wf[w, i])

        @pl.when(lax.div(i, half) == chip)
        def _():
            if side == 0:
                add(0)

                @pl.when(jnp.logical_not(is_dec))
                def _():
                    add(1)
                    add(2)
            else:
                add(1)
                add(2)

    def both_sides(f, i):
        f(0, i)
        pl.when(is_dec)(lambda: f(1, i))

    def ring_step(k, multiply):
        for which in range(2):
            def go():
                for way in WAYS:
                    ring(which, way, k - 1).wait_recv()
                    if hops(way) == half:
                        ring(which, way, k).start()
                    else:
                        @pl.when(k < half)
                        def _():
                            ring(which, way, k).start()
            if which == 0:
                go()
            else:
                pl.when(is_dec)(go)
        for i in (lax.rem(z + N_TP + 1 - k, N_TP), lax.rem(z + k - 1, N_TP)):
            both_sides(take, i)
            if multiply:
                both_sides(near, i)

    def early(k, carry):
        ring_step(k, False)
        return carry

    def later(k, carry):
        ring_step(k, True)
        return carry

    both_sides(take, z)
    lax.fori_loop(2, 4, early, 0)
    for w in range(3):
        weight_mate(w).wait_recv()
    for distance in (0, 1, -1, 2, -2):
        both_sides(near, lax.rem(z + distance + N_TP, N_TP))
    lax.fori_loop(4, 6, later, 0)
    weight_far(0).wait_recv()
    weight_relay(0).start()
    lax.fori_loop(6, half + 1, later, 0)

    def ring_end(side):
        for way in WAYS:
            if hops(way) == half:
                ring(side, way, half).wait_recv()
        opposite = lax.rem(z + half, N_TP)
        take(side, opposite)
        near(side, opposite)

    ring_end(0)
    pl.when(is_dec)(lambda: ring_end(1))
    weight_far(1).wait_recv()
    weight_relay(1).start()

    def row_scale(side):
        mean = jnp.sum(sq[side], axis=1, keepdims=True) * (1.0 / (N_TP * WIDE))
        return jnp.broadcast_to(lax.rsqrt(mean + EPSILON), (ROWS, 128))

    stream_inverse = row_scale(0)
    inv[0] = stream_inverse
    inv[1] = stream_inverse

    @pl.when(is_dec)
    def _():
        inv[1] = row_scale(1)

    def give_far(side):
        return remote(
            xm.at[side, pl.ds(4 * far, 4)], x_all.at[side, :, d], ex_s.at[side, 0], ex_r.at[side, 0], {"dp": far}
        )

    def give_far_mate(side):
        return remote(
            xm.at[side, pl.ds(4 * far_mate, 4)], x_rel.at[side], ex_s.at[side, 1], ex_r.at[side, 1], {"dp": far}
        )

    def give_mate(side):
        return remote(
            xm.at[side, pl.ds(4 * mate, 4)], x_all.at[side, :, d], ex_s.at[side, 2], ex_r.at[side, 2], {"dp": mate}
        )

    def relay_mate(side):
        return remote(
            x_rel.at[side], x_all.at[side, :, far], ex_s.at[side, 3], ex_r.at[side, 3], {"dp": mate}
        )

    def keep_own(side):
        return pltpu.make_async_copy(xm.at[side, pl.ds(4 * d, 4)], x_all.at[side, :, d], loc.at[4 + side])

    def start_exchange(side):
        give_far_mate(side).start()
        give_far(side).start()
        give_mate(side).start()
        keep_own(side).start()

    start_exchange(0)

    def project(w):
        side = 0 if w == 0 else src
        begin = (1 - chip) * half

        def step(i, total):
            return total + dot_nn(xm[side, begin + i], wf[w, begin + i])

        acc[w] = lax.fori_loop(0, half, step, acc[w])

    for w in range(2):
        weight_relay(w).wait_recv()
        project(w)

    row = lax.broadcasted_iota(jnp.int32, (ROWS, ROWS), 0)
    col = lax.broadcasted_iota(jnp.int32, (ROWS, ROWS), 1)
    row_sample = lax.shift_right_logical(row, 5)
    col_sample = jnp.where(
        is_dec, jnp.bitwise_and(lax.shift_right_logical(col, 2), 3), lax.shift_right_logical(col, 5)
    )
    col_slot = jnp.where(
        is_dec, lax.shift_right_logical(col, 4) * 4 + jnp.bitwise_and(col, 3), jnp.bitwise_and(col, 31)
    )
    wanted = jnp.zeros((ROWS, ROWS), jnp.int32)
    key_len = jnp.zeros((ROWS, ROWS), jnp.int32)
    query_len = jnp.zeros((ROWS, ROWS), jnp.int32)
    for m in range(4):
        chosen = jnp.where(is_dec, assign[m], m)
        length = jnp.where(is_dec, dec_len[m], enc_len[m])
        wanted = jnp.where(row_sample == m, chosen, wanted)
        key_len = jnp.where(col_sample == m, enc_len[m], key_len)
        query_len = jnp.where(row_sample == m, length, query_len)
    live = jnp.logical_and(wanted == col_sample, col_slot < key_len)
    row_live = (jnp.bitwise_and(row, 31) < query_len).astype(F32)[:, 0:HEAD_DIM]

    q_scale = jnp.concatenate([inv[0], inv[0]], axis=1)
    s_scale = jnp.concatenate([inv[1], inv[1]], axis=1)
    qkv[0] = (acc[0] * q_scale).astype(BF16)
    qkv[1] = (acc[1] * s_scale).astype(BF16)
    scale = HEAD_DIM**-0.5
    for h in range(WIDE // HEAD_DIM):
        at = slice(h * HEAD_DIM, (h + 1) * HEAD_DIM)
        scores = jnp.where(live, dot_nt(qkv[0, :, at], qkv[1, :, at]) * scale, -1e30)
        raised = jnp.exp(scores - jnp.max(scores, axis=1, keepdims=True))
        soft[h] = raised / jnp.sum(raised, axis=1, keepdims=True)
        up[:, at] = (cot[:, at].astype(F32) * row_live).astype(BF16)

    def add_values(i):
        acc[2] = acc[2] + dot_nn(xm[src, i], wf[2, i])

    for quarter in range(4):
        weight_far(2, quarter).wait_recv()
        weight_relay(2, quarter).start()
        add_values(4 * far + quarter)
        if quarter > 0:
            weight_relay(2, quarter - 1).wait_recv()
            add_values(4 * far_mate + quarter - 1)
    weight_relay(2, 3).wait_recv()
    add_values(4 * far_mate + 3)
    qkv[2] = (acc[2] * jnp.concatenate([inv[1], inv[1]], axis=1)).astype(BF16)

    for h in range(WIDE // HEAD_DIM):
        at = slice(h * HEAD_DIM, (h + 1) * HEAD_DIM)
        qh, kh, vh, upstream = qkv[0, :, at], qkv[1, :, at], qkv[2, :, at], up[:, at]
        weights = soft[h]
        probs = weights.astype(BF16)
        mix_o[:, at] = (dot_nn(probs, vh) * row_live).astype(BF16)
        grad_weights = dot_nt(upstream, vh)
        inner = jnp.sum(grad_weights * weights, axis=1, keepdims=True)
        grad_scores = (weights * (grad_weights - inner) * scale).astype(BF16)
        g_own[0, :, at] = (dot_nn(grad_scores, kh) * inv[0][:, 0:HEAD_DIM]).astype(BF16)
        g_own[1, :, at] = (dot_tn(grad_scores, qh) * inv[1][:, 0:HEAD_DIM]).astype(BF16)
        g_own[2, :, at] = (dot_tn(probs, upstream) * inv[1][:, 0:HEAD_DIM]).astype(BF16)

    def back(i):
        grad_q = dot_nt(g_own[0], wf[0, i])
        grad_s = dot_nt(g_own[1], wf[1, i]) + dot_nt(g_own[2], wf[2, i])
        part[0, i] = jnp.where(is_dec, grad_q, grad_q + grad_s).astype(BF16)
        part[1, i] = grad_s.astype(BF16)

    def chain_at(way_hops, direction, k):
        ahead = way_hops + 1 - k
        return lax.rem(z + ahead, N_TP) if direction == 0 else lax.rem(z - ahead + N_TP, N_TP)

    def chain(side, way, k, first):
        direction, chunk = way
        rows = pl.ds(chunk * HALF, HALF)
        begin = (
            part.at[side, chain_at(hops(way), direction, k), rows] if first else rs.at[side, direction, k - 2, rows]
        )
        return remote(
            begin, rs.at[side, direction, k - 1, rows],
            rs_s.at[side, direction, chunk, k - 1], rs_r.at[side, direction, chunk, k - 1], around[direction],
        )

    def chain_dots(direction, k, first):
        begin = dots if first else rsd.at[direction, k - 2]
        return remote(begin, rsd.at[direction, k - 1], d_s.at[direction, k - 1], d_r.at[direction, k - 1], around[direction])

    def chain_first(way):
        pl.when(is_dec)(lambda: chain(1, way, 1, True).start())
        chain(0, way, 1, True).start()

    back(lax.rem(z + half, N_TP))
    chain_first((0, 0))
    chain_first((1, 1))
    back(lax.rem(z + half - 1, N_TP))
    chain_first((0, 1))
    back(lax.rem(z + half + 1, N_TP))
    chain_first((1, 0))

    def g_far():
        return remote(g_own, g_all.at[:, d], ex_s.at[2, 0], ex_r.at[2, 0], {"dp": far})

    def g_mate():
        return remote(g_own, g_all.at[:, d], ex_s.at[2, 2], ex_r.at[2, 2], {"dp": mate})

    def g_relay():
        return remote(g_all.at[:, far], g_all.at[:, far], ex_s.at[2, 3], ex_r.at[2, 3], {"dp": mate})

    g_keep = pltpu.make_async_copy(g_own, g_all.at[:, d], loc.at[6])
    g_far().start()
    g_mate().start()
    g_keep.start()
    pl.when(is_dec)(lambda: start_exchange(1))

    shared_dot = g_own[1].astype(F32) * acc[1] + g_own[2].astype(F32) * acc[2]
    query_dot = g_own[0].astype(F32) * acc[0]
    diagonal = row == col
    for side, total in ((0, jnp.where(is_dec, query_dot, query_dot + shared_dot)), (1, shared_dot)):
        column = jnp.sum(total, axis=1, keepdims=True) * (1.0 / (N_TP * WIDE)) * inv[side] * inv[side]
        across = jnp.sum(jnp.where(diagonal, column, 0.0), axis=0, keepdims=True)
        dots[:, side * 128 : (side + 1) * 128] = jnp.broadcast_to(across, (8, 128))
    chain_dots(0, 1, True).start()
    chain_dots(1, 1, True).start()

    def chain_step(k, _):
        back(lax.rem(z + half - k, N_TP))

        @pl.when(k < half)
        def _():
            back(lax.rem(z + half + k, N_TP))

        def go(side):
            for way in WAYS:
                direction, chunk = way
                last = hops(way)

                def one():
                    chain(side, way, k - 1, True).wait_recv()
                    rows = pl.ds(chunk * HALF, HALF)
                    target = chain_at(last, direction, k)
                    rs[side, direction, k - 2, rows] = (
                        rs[side, direction, k - 2, rows].astype(F32) + part[side, target, rows].astype(F32)
                    ).astype(BF16)
                    chain(side, way, k, False).start()

                if last == N_TP // 2:
                    one()
                else:
                    pl.when(k < N_TP // 2)(one)

        pl.when(is_dec)(lambda: go(1))
        go(0)
        for direction in range(2):
            def one_dots():
                chain_dots(direction, k - 1, True).wait_recv()
                rsd[direction, k - 2] = rsd[direction, k - 2] + dots[...]
                chain_dots(direction, k, False).start()

            if direction == 0:
                one_dots()
            else:
                pl.when(k < N_TP // 2)(one_dots)
        return 0

    def relay(side):
        give_far_mate(side).wait_recv()
        relay_mate(side).start()

    def settled(side):
        give_far(side).wait_recv()
        give_mate(side).wait_recv()
        relay_mate(side).wait_recv()
        keep_own(side).wait()

    def weight_gradient(w, side, out):
        for j in range(4):
            left_side = x_all[side, j].reshape(N_DP * ROWS, WIDE)
            right_side = g_all[w].reshape(N_DP * ROWS, WIDE)
            out[j] = dot_tn(left_side, right_side).astype(BF16)

    lax.fori_loop(2, 6, chain_step, 0)
    g_far().wait_recv()
    g_relay().start()
    relay(0)
    lax.fori_loop(6, 8, chain_step, 0)
    settled(0)
    g_mate().wait_recv()
    g_relay().wait_recv()
    g_keep.wait()
    weight_gradient(0, 0, dq_o)
    lax.fori_loop(8, N_TP // 2 + 1, chain_step, 0)
    chain_dots(0, N_TP // 2, True).wait_recv()
    chain_dots(1, N_TP // 2 - 1, True).wait_recv()
    summed = rsd[0, N_TP // 2 - 1] + rsd[1, N_TP // 2 - 2] + dots[...]

    def arrived(side, chunk):
        rows = pl.ds(chunk * HALF, HALF)
        total = part[side, z, rows].astype(F32)
        for direction in range(2):
            way = (direction, chunk)
            chain(side, way, hops(way), True).wait_recv()
            total = total + rs[side, direction, hops(way) - 1, rows].astype(F32)
        return total

    def column_of(side):
        across = jnp.broadcast_to(summed[0:1, side * 128 : (side + 1) * 128], (ROWS, ROWS))
        return jnp.sum(jnp.where(diagonal, across, 0.0), axis=1, keepdims=True)

    here = pl.ds(pl.multiple_of(z * WIDE, WIDE), WIDE)

    def give_memory(i):
        return remote(h_out.at[i], h_in.at[s - FIRST_DECODER], h_s.at[i], h_r.at[0], {"section": i})

    @pl.when(is_dec)
    def _():
        gain = fgain[0:1, here]
        column = column_of(1)
        for chunk in range(2):
            rows = slice(chunk * HALF, (chunk + 1) * HALF)
            value = gain * arrived(1, chunk) - gat[1, z, rows].astype(F32) * column[rows]
            h_out[chunk * 4 : chunk * 4 + 4] = value.reshape(4, PIECE, WIDE)
        for i in range(N_SECTION):
            @pl.when(s != i)
            def _():
                give_memory(i).start()
        pltpu.make_async_copy(h_out.at[s], h_in.at[s - FIRST_DECODER], h_r.at[0]).start()

    gain_here = lgain[0:1, here]
    stream_column = column_of(0)
    for chunk in range(2):
        rows = slice(chunk * HALF, (chunk + 1) * HALF)
        value = gain_here * arrived(0, chunk) - stream[rows].astype(F32) * stream_column[rows]
        sg_o[rows] = value.astype(BF16)

    pl.when(is_dec)(lambda: relay(1))
    pl.when(is_dec)(lambda: settled(1))
    weight_gradient(1, src, dk_o)
    weight_gradient(2, src, dv_o)

    pltpu.make_async_copy(h_in, h_in, h_r.at[0]).wait()
    mg_o[...] = h_in[0] + h_in[1] + h_in[2] + h_in[3]

    def drain(which):
        for way in WAYS:
            def step(k, _):
                ring(which, way, k).wait_send()
                chain(which, way, k, True).wait_send()
                return 0

            lax.fori_loop(1, hops(way) + 1, step, 0)

    drain(0)
    pl.when(is_dec)(lambda: drain(1))
    for w in range(3):
        weight_mate(w).wait_send()
        for quarter in range(4 if w == 2 else 1):
            weight_far(w, quarter).wait_send()
            weight_relay(w, quarter).wait_send()
    for i in range(N_SECTION - FIRST_DECODER):
        @pl.when(s != FIRST_DECODER + i)
        def _():
            mem_send(i).wait_send()

    def drain_exchange(side):
        give_far(side).wait_send()
        give_far_mate(side).wait_send()
        give_mate(side).wait_send()
        relay_mate(side).wait_send()

    drain_exchange(0)
    pl.when(is_dec)(lambda: drain_exchange(1))
    g_far().wait_send()
    g_mate().wait_send()
    g_relay().wait_send()
    for direction in range(2):
        def step(k, _):
            chain_dots(direction, k, True).wait_send()
            return 0

        lax.fori_loop(1, N_TP // 2 + 1 - direction, step, 0)

    @pl.when(is_dec)
    def _():
        for i in range(N_SECTION):
            @pl.when(s != i)
            def _():
                give_memory(i).wait_send()


def hand_out(mix, sg, mg, dq, dk, dv, mix_o, sg_o, mg_o, dq_o, dk_o, dv_o):
    mix_o[...] = mix[...]
    sg_o[...] = sg[...]
    for n in range(4):
        mg_o[n] = mg[n * 4 : n * 4 + 4].astype(BF16)
    dq_o[...] = dq[...]
    dk_o[...] = dk[...]
    dv_o[...] = dv[...]


def shards(
    stream, memory_hidden, layer_gain, final_gain, query_weight, key_weight, value_weight,
    cotangent, encoder_lengths, decoder_lengths, assignment,
):
    vmem = pl.BlockSpec(memory_space=pltpu.VMEM)
    hbm = pl.BlockSpec(memory_space=pl.ANY)
    smem = pl.BlockSpec(memory_space=pltpu.SMEM)
    dma = pltpu.SemaphoreType.DMA
    outs = pl.pallas_call(
        body,
        name="relay",
        out_shape=(
            jax.ShapeDtypeStruct((ROWS, WIDE), BF16),
            jax.ShapeDtypeStruct((ROWS, WIDE), BF16),
            jax.ShapeDtypeStruct((PIECE, WIDE), F32),
            jax.ShapeDtypeStruct((4, WIDE, WIDE), BF16),
            jax.ShapeDtypeStruct((4, WIDE, WIDE), BF16),
            jax.ShapeDtypeStruct((4, WIDE, WIDE), BF16),
        ),
        in_specs=[vmem, vmem, vmem, vmem, hbm, hbm, hbm, vmem, smem, smem, smem],
        out_specs=(vmem,) * 6,
        scratch_shapes=[
            pltpu.VMEM((PIECE, WIDE), BF16),
            pltpu.VMEM((2, N_TP, ROWS, WIDE), BF16),
            pltpu.VMEM((2, N_TP, ROWS, WIDE), BF16),
            pltpu.VMEM((2, ROWS, WIDE), F32),
            pltpu.VMEM((3, N_TP, WIDE, WIDE), BF16),
            pltpu.VMEM((3, ROWS, WIDE), F32),
            pltpu.VMEM((2, ROWS, 128), F32),
            pltpu.VMEM((3, ROWS, WIDE), BF16),
            pltpu.VMEM((4, ROWS, ROWS), F32),
            pltpu.VMEM((ROWS, WIDE), BF16),
            pltpu.VMEM((3, ROWS, WIDE), BF16),
            pltpu.VMEM((3, N_DP, ROWS, WIDE), BF16),
            pltpu.VMEM((2, 4, N_DP, ROWS, WIDE), BF16),
            pltpu.VMEM((2, 4, ROWS, WIDE), BF16),
            pltpu.VMEM((2, N_TP, ROWS, WIDE), BF16),
            pltpu.VMEM((2, 2, N_TP // 2, ROWS, WIDE), BF16),
            pltpu.VMEM((8, 256), F32),
            pltpu.VMEM((2, N_TP // 2, 8, 256), F32),
            pltpu.VMEM((N_SECTION, PIECE, WIDE), F32),
            pltpu.VMEM((N_SECTION - FIRST_DECODER, PIECE, WIDE), F32),
            dma((2, 2, 2, 8)), dma((2, 2, 2, 8)),
            dma((6,)), dma((6,)), dma((3,)), dma((3,)), dma((6,)), dma((6,)),
            dma((4,)), dma((1,)),
            dma((3, 4)), dma((3, 4)),
            dma((2, 2, 2, 8)), dma((2, 2, 2, 8)),
            dma((2, 8)), dma((2, 8)),
            dma((8,)), dma((1,)),
            dma((7,)),
        ],
        compiler_params=pltpu.CompilerParams(
            collective_id=0, has_side_effects=True, vmem_limit_bytes=60 * 1024 * 1024
        ),
    )(
        stream.reshape(ROWS, WIDE),
        memory_hidden,
        layer_gain,
        final_gain.reshape(1, N_TP * WIDE),
        query_weight.reshape(4, WIDE, WIDE),
        key_weight.reshape(4, WIDE, WIDE),
        value_weight.reshape(4, WIDE, WIDE),
        cotangent.reshape(ROWS, WIDE),
        encoder_lengths,
        decoder_lengths,
        assignment.reshape(4),
    )
    mixture, stream_grad, memory_grad, dq, dk, dv = pl.pallas_call(
        hand_out,
        name="hand_out",
        out_shape=(
            jax.ShapeDtypeStruct((ROWS, WIDE), BF16),
            jax.ShapeDtypeStruct((ROWS, WIDE), BF16),
            jax.ShapeDtypeStruct((4, 4, WIDE), BF16),
            jax.ShapeDtypeStruct((4, WIDE, WIDE), BF16),
            jax.ShapeDtypeStruct((4, WIDE, WIDE), BF16),
            jax.ShapeDtypeStruct((4, WIDE, WIDE), BF16),
        ),
        in_specs=[vmem] * 6,
        out_specs=(vmem,) * 6,
    )(*outs)
    rows = (1, 4, 32, WIDE)
    square = (1, 4 * WIDE, WIDE)
    return (
        mixture.reshape(rows),
        stream_grad.reshape(rows),
        memory_grad,
        dq.reshape(square),
        dk.reshape(square),
        dv.reshape(square),
    )


def solution(mesh):
    tokens = P("section", "dp", None, "tp")
    weight = P("section", "dp", "tp")
    memory = P("dp", "section", "tp")
    return jax.shard_map(
        shards,
        mesh=mesh,
        in_specs=(
            tokens, memory, P("section", None), P(), weight, weight, weight, tokens, P("dp"), P("dp"), P("dp", None),
        ),
        out_specs=(tokens, tokens, memory, weight, weight, weight),
        check_vma=False,
    )
```

```python
import functools

import jax
import jax.numpy as jnp
from jax import lax
from jax.experimental import pallas as pl
from jax.experimental.pallas import tpu as pltpu
from jax.sharding import PartitionSpec as P

MESH = pl.DeviceIdType.MESH
F32 = jnp.float32
BF16 = jnp.bfloat16
EPSILON = 1e-06
HEAD_DIM = 64
N_SECTION = 8
N_TP = 16
N_DP = 4
ROWS = 128
WIDE = 256
CHUNKS = 4
HALF = ROWS // CHUNKS
PIECE = 16
FIRST_DECODER = N_SECTION // 2
WAYS = [(direction, chunk) for chunk in range(CHUNKS) for direction in range(2)]


def dot_nn(a, b):
    return lax.dot_general(a, b, (((1,), (0,)), ((), ())), preferred_element_type=F32)


def dot_nt(a, b):
    return lax.dot_general(a, b, (((1,), (1,)), ((), ())), preferred_element_type=F32)


def dot_tn(a, b):
    return lax.dot_general(a, b, (((0,), (0,)), ((), ())), preferred_element_type=F32)


def hops(way):
    return N_TP // 2 if way[0] == way[1] % 2 else N_TP // 2 - 1


def body(
    stream, mem, lgain, fgain, wq, wk, wv, cot, enc_len, dec_len, assign,
    mix_o, sg_o, mg_o, dq_o, dk_o, dv_o,
    piece, gat, xm, sq, wf, acc, inv, qkv, soft, up, g_own, g_all, x_all, x_rel, part, rs, dots, rsd, h_out, h_in,
    ag_s, ag_r, wy_s, wy_r, wc_s, wc_r, wr_s, wr_r, m_s, m_r, ex_s, ex_r, rs_s, rs_r, d_s, d_r, h_s, h_r, loc,
):
    s = lax.axis_index("section")
    z = lax.axis_index("tp")
    d = lax.axis_index("dp")
    is_dec = s >= FIRST_DECODER
    src = jnp.where(is_dec, 1, 0)
    core = lax.rem(d, 2)
    chip = lax.div(d, 2)
    mate = d + 1 - 2 * core
    far = lax.rem(d + 2, N_DP)
    far_mate = lax.rem(mate + 2, N_DP)
    right = {"tp": lax.rem(z + 1, N_TP)}
    left = {"tp": lax.rem(z + N_TP - 1, N_TP)}
    around = [right, left]

    def remote(a, b, ss, rr, to):
        return pltpu.make_async_remote_copy(
            src_ref=a, dst_ref=b, send_sem=ss, recv_sem=rr, device_id=to, device_id_type=MESH
        )

    barrier = pltpu.get_barrier_semaphore()
    for to in (right, left, {"dp": mate}, {"dp": far}):
        pl.semaphore_signal(barrier, inc=1, device_id=to, device_id_type=MESH)
    for other in range(1, N_SECTION):
        pl.semaphore_signal(
            barrier, inc=1, device_id={"section": lax.rem(s + other, N_SECTION)}, device_id_type=MESH
        )

    own = [
        pltpu.make_async_copy(stream, gat.at[0, z], loc.at[0]),
        pltpu.make_async_copy(wq, wf.at[0, pl.ds(4 * d, 4)], loc.at[1]),
        pltpu.make_async_copy(wk, wf.at[1, pl.ds(4 * d, 4)], loc.at[2]),
        pltpu.make_async_copy(wv, wf.at[2, pl.ds(4 * d, 4)], loc.at[3]),
    ]
    for c in own[1:]:
        c.start()
    own[0].start()
    piece[...] = jnp.concatenate([mem[n].astype(F32) for n in range(4)], axis=0).astype(BF16)
    for side in range(2):
        sq[side] = jnp.zeros((ROWS, WIDE), F32)
    for w in range(3):
        acc[w] = jnp.zeros((ROWS, WIDE), F32)
    pl.semaphore_wait(barrier, N_SECTION + 3)

    def ring(which, way, k):
        direction, chunk = way
        rows = pl.ds(chunk * HALF, HALF)
        back = k - 1 if direction == 0 else 1 - k
        at = lax.rem(z - back + N_TP, N_TP)
        return remote(
            gat.at[which, at, rows], gat.at[which, at, rows],
            ag_s.at[which, direction, chunk, k - 1], ag_r.at[which, direction, chunk, k - 1],
            around[direction],
        )

    def weight_part(w, quarter, owner):
        if w < 2:
            return wf.at[w, pl.ds(4 * owner, 4)], w
        return wf.at[w, pl.ds(4 * owner + quarter, 1)], w + quarter

    def weight_far(w, quarter=0):
        block, at = weight_part(w, quarter, d)
        return remote(block, block, wy_s.at[at], wy_r.at[at], {"dp": far})

    def weight_mate(w):
        return remote(
            wf.at[w, pl.ds(4 * d, 4)], wf.at[w, pl.ds(4 * d, 4)], wc_s.at[w], wc_r.at[w], {"dp": mate}
        )

    def weight_relay(w, quarter=0):
        block, at = weight_part(w, quarter, far)
        return remote(block, block, wr_s.at[at], wr_r.at[at], {"dp": mate})

    def mem_send(i):
        return remote(
            piece, gat.at[1, z, pl.ds(s * PIECE, PIECE)], m_s.at[i], m_r.at[0], {"section": FIRST_DECODER + i}
        )

    def mem_keep():
        return pltpu.make_async_copy(piece, gat.at[1, z, pl.ds(s * PIECE, PIECE)], m_r.at[0])

    for i in range(N_SECTION - FIRST_DECODER):
        @pl.when(s != FIRST_DECODER + i)
        def _():
            mem_send(i).start()

    @pl.when(is_dec)
    def _():
        mem_keep().start()

    own[0].wait()
    for way in WAYS:
        ring(0, way, 1).start()
    for w in range(3):
        own[1 + w].wait()
        for quarter in range(4 if w == 2 else 1):
            weight_far(w, quarter).start()

    for w in range(3):
        weight_mate(w).start()

    @pl.when(is_dec)
    def _():
        pltpu.make_async_copy(gat.at[1, z], gat.at[1, z], m_r.at[0]).wait()
        for way in WAYS:
            ring(1, way, 1).start()

    half = N_TP // 2

    def take(side, i):
        value = gat[side, i].astype(F32)
        gain = (lgain, fgain)[side][0:1, pl.ds(pl.multiple_of(i * WIDE, WIDE), WIDE)]
        xm[side, i] = (value * gain).astype(BF16)
        sq[side] = sq[side] + value * value

    def near(side, i):
        def add(w):
            acc[w] = acc[w] + dot_nn(xm[side, i], wf[w, i])

        @pl.when(lax.div(i, half) == chip)
        def _():
            if side == 0:
                add(0)

                @pl.when(jnp.logical_not(is_dec))
                def _():
                    add(1)
                    add(2)
            else:
                add(1)
                add(2)

    def both_sides(f, i):
        f(0, i)
        pl.when(is_dec)(lambda: f(1, i))

    def ring_step(k, multiply):
        for which in range(2):
            def go():
                for way in WAYS:
                    ring(which, way, k - 1).wait_recv()
                    if hops(way) == half:
                        ring(which, way, k).start()
                    else:
                        @pl.when(k < half)
                        def _():
                            ring(which, way, k).start()
            if which == 0:
                go()
            else:
                pl.when(is_dec)(go)
        for i in (lax.rem(z + N_TP + 1 - k, N_TP), lax.rem(z + k - 1, N_TP)):
            both_sides(take, i)
            if multiply:
                both_sides(near, i)

    def early(k, carry):
        ring_step(k, False)
        return carry

    def later(k, carry):
        ring_step(k, True)
        return carry

    both_sides(take, z)
    lax.fori_loop(2, 4, early, 0)
    for w in range(3):
        weight_mate(w).wait_recv()
    for distance in (0, 1, -1, 2, -2):
        both_sides(near, lax.rem(z + distance + N_TP, N_TP))
    lax.fori_loop(4, 6, later, 0)
    weight_far(0).wait_recv()
    weight_relay(0).start()
    lax.fori_loop(6, half + 1, later, 0)

    def ring_end(side):
        for way in WAYS:
            if hops(way) == half:
                ring(side, way, half).wait_recv()
        opposite = lax.rem(z + half, N_TP)
        take(side, opposite)
        near(side, opposite)

    ring_end(0)
    pl.when(is_dec)(lambda: ring_end(1))
    weight_far(1).wait_recv()
    weight_relay(1).start()

    def row_scale(side):
        mean = jnp.sum(sq[side], axis=1, keepdims=True) * (1.0 / (N_TP * WIDE))
        return jnp.broadcast_to(lax.rsqrt(mean + EPSILON), (ROWS, 128))

    stream_inverse = row_scale(0)
    inv[0] = stream_inverse
    inv[1] = stream_inverse

    @pl.when(is_dec)
    def _():
        inv[1] = row_scale(1)

    def give_far(side):
        return remote(
            xm.at[side, pl.ds(4 * far, 4)], x_all.at[side, :, d], ex_s.at[side, 0], ex_r.at[side, 0], {"dp": far}
        )

    def give_far_mate(side):
        return remote(
            xm.at[side, pl.ds(4 * far_mate, 4)], x_rel.at[side], ex_s.at[side, 1], ex_r.at[side, 1], {"dp": far}
        )

    def give_mate(side):
        return remote(
            xm.at[side, pl.ds(4 * mate, 4)], x_all.at[side, :, d], ex_s.at[side, 2], ex_r.at[side, 2], {"dp": mate}
        )

    def relay_mate(side):
        return remote(
            x_rel.at[side], x_all.at[side, :, far], ex_s.at[side, 3], ex_r.at[side, 3], {"dp": mate}
        )

    def keep_own(side):
        return pltpu.make_async_copy(xm.at[side, pl.ds(4 * d, 4)], x_all.at[side, :, d], loc.at[4 + side])

    def start_exchange(side):
        give_far_mate(side).start()
        give_far(side).start()
        give_mate(side).start()
        keep_own(side).start()

    start_exchange(0)

    def project(w):
        side = 0 if w == 0 else src
        begin = (1 - chip) * half

        def step(i, total):
            return total + dot_nn(xm[side, begin + i], wf[w, begin + i])

        acc[w] = lax.fori_loop(0, half, step, acc[w])

    for w in range(2):
        weight_relay(w).wait_recv()
        project(w)

    row = lax.broadcasted_iota(jnp.int32, (ROWS, ROWS), 0)
    col = lax.broadcasted_iota(jnp.int32, (ROWS, ROWS), 1)
    row_sample = lax.shift_right_logical(row, 5)
    col_sample = jnp.where(
        is_dec, jnp.bitwise_and(lax.shift_right_logical(col, 2), 3), lax.shift_right_logical(col, 5)
    )
    col_slot = jnp.where(
        is_dec, lax.shift_right_logical(col, 4) * 4 + jnp.bitwise_and(col, 3), jnp.bitwise_and(col, 31)
    )
    wanted = jnp.zeros((ROWS, ROWS), jnp.int32)
    key_len = jnp.zeros((ROWS, ROWS), jnp.int32)
    query_len = jnp.zeros((ROWS, ROWS), jnp.int32)
    for m in range(4):
        chosen = jnp.where(is_dec, assign[m], m)
        length = jnp.where(is_dec, dec_len[m], enc_len[m])
        wanted = jnp.where(row_sample == m, chosen, wanted)
        key_len = jnp.where(col_sample == m, enc_len[m], key_len)
        query_len = jnp.where(row_sample == m, length, query_len)
    live = jnp.logical_and(wanted == col_sample, col_slot < key_len)
    row_live = (jnp.bitwise_and(row, 31) < query_len).astype(F32)[:, 0:HEAD_DIM]

    q_scale = jnp.concatenate([inv[0], inv[0]], axis=1)
    s_scale = jnp.concatenate([inv[1], inv[1]], axis=1)
    qkv[0] = (acc[0] * q_scale).astype(BF16)
    qkv[1] = (acc[1] * s_scale).astype(BF16)
    scale = HEAD_DIM**-0.5
    for h in range(WIDE // HEAD_DIM):
        at = slice(h * HEAD_DIM, (h + 1) * HEAD_DIM)
        scores = jnp.where(live, dot_nt(qkv[0, :, at], qkv[1, :, at]) * scale, -1e30)
        raised = jnp.exp(scores - jnp.max(scores, axis=1, keepdims=True))
        soft[h] = raised / jnp.sum(raised, axis=1, keepdims=True)
        up[:, at] = (cot[:, at].astype(F32) * row_live).astype(BF16)

    def add_values(i):
        acc[2] = acc[2] + dot_nn(xm[src, i], wf[2, i])

    for quarter in range(4):
        weight_far(2, quarter).wait_recv()
        weight_relay(2, quarter).start()
        add_values(4 * far + quarter)
        if quarter > 0:
            weight_relay(2, quarter - 1).wait_recv()
            add_values(4 * far_mate + quarter - 1)
    weight_relay(2, 3).wait_recv()
    add_values(4 * far_mate + 3)
    qkv[2] = (acc[2] * jnp.concatenate([inv[1], inv[1]], axis=1)).astype(BF16)

    for h in range(WIDE // HEAD_DIM):
        at = slice(h * HEAD_DIM, (h + 1) * HEAD_DIM)
        qh, kh, vh, upstream = qkv[0, :, at], qkv[1, :, at], qkv[2, :, at], up[:, at]
        weights = soft[h]
        probs = weights.astype(BF16)
        mix_o[:, at] = (dot_nn(probs, vh) * row_live).astype(BF16)
        grad_weights = dot_nt(upstream, vh)
        inner = jnp.sum(grad_weights * weights, axis=1, keepdims=True)
        grad_scores = (weights * (grad_weights - inner) * scale).astype(BF16)
        g_own[0, :, at] = (dot_nn(grad_scores, kh) * inv[0][:, 0:HEAD_DIM]).astype(BF16)
        g_own[1, :, at] = (dot_tn(grad_scores, qh) * inv[1][:, 0:HEAD_DIM]).astype(BF16)
        g_own[2, :, at] = (dot_tn(probs, upstream) * inv[1][:, 0:HEAD_DIM]).astype(BF16)

    def back(i):
        grad_q = dot_nt(g_own[0], wf[0, i])
        grad_s = dot_nt(g_own[1], wf[1, i]) + dot_nt(g_own[2], wf[2, i])
        part[0, i] = jnp.where(is_dec, grad_q, grad_q + grad_s).astype(BF16)
        part[1, i] = grad_s.astype(BF16)

    def chain_at(way_hops, direction, k):
        ahead = way_hops + 1 - k
        return lax.rem(z + ahead, N_TP) if direction == 0 else lax.rem(z - ahead + N_TP, N_TP)

    def chain(side, way, k, first):
        direction, chunk = way
        rows = pl.ds(chunk * HALF, HALF)
        begin = (
            part.at[side, chain_at(hops(way), direction, k), rows] if first else rs.at[side, direction, k - 2, rows]
        )
        return remote(
            begin, rs.at[side, direction, k - 1, rows],
            rs_s.at[side, direction, chunk, k - 1], rs_r.at[side, direction, chunk, k - 1], around[direction],
        )

    def chain_dots(direction, k, first):
        begin = dots if first else rsd.at[direction, k - 2]
        return remote(begin, rsd.at[direction, k - 1], d_s.at[direction, k - 1], d_r.at[direction, k - 1], around[direction])

    def chain_first(direction, long):
        for way in WAYS:
            if way[0] == direction and (hops(way) == half) == long:
                pl.when(is_dec)(lambda: chain(1, way, 1, True).start())
                chain(0, way, 1, True).start()

    back(lax.rem(z + half, N_TP))
    chain_first(0, True)
    chain_first(1, True)
    back(lax.rem(z + half - 1, N_TP))
    chain_first(0, False)
    back(lax.rem(z + half + 1, N_TP))
    chain_first(1, False)

    def g_far():
        return remote(g_own, g_all.at[:, d], ex_s.at[2, 0], ex_r.at[2, 0], {"dp": far})

    def g_mate():
        return remote(g_own, g_all.at[:, d], ex_s.at[2, 2], ex_r.at[2, 2], {"dp": mate})

    def g_relay():
        return remote(g_all.at[:, far], g_all.at[:, far], ex_s.at[2, 3], ex_r.at[2, 3], {"dp": mate})

    g_keep = pltpu.make_async_copy(g_own, g_all.at[:, d], loc.at[6])
    g_far().start()
    g_mate().start()
    g_keep.start()
    pl.when(is_dec)(lambda: start_exchange(1))

    shared_dot = g_own[1].astype(F32) * acc[1] + g_own[2].astype(F32) * acc[2]
    query_dot = g_own[0].astype(F32) * acc[0]
    diagonal = row == col
    for side, total in ((0, jnp.where(is_dec, query_dot, query_dot + shared_dot)), (1, shared_dot)):
        column = jnp.sum(total, axis=1, keepdims=True) * (1.0 / (N_TP * WIDE)) * inv[side] * inv[side]
        across = jnp.sum(jnp.where(diagonal, column, 0.0), axis=0, keepdims=True)
        dots[:, side * 128 : (side + 1) * 128] = jnp.broadcast_to(across, (8, 128))
    chain_dots(0, 1, True).start()
    chain_dots(1, 1, True).start()

    def chain_step(k, _):
        back(lax.rem(z + half - k, N_TP))

        @pl.when(k < half)
        def _():
            back(lax.rem(z + half + k, N_TP))

        def go(side):
            for way in WAYS:
                direction, chunk = way
                last = hops(way)

                def one():
                    chain(side, way, k - 1, True).wait_recv()
                    rows = pl.ds(chunk * HALF, HALF)
                    target = chain_at(last, direction, k)
                    rs[side, direction, k - 2, rows] = (
                        rs[side, direction, k - 2, rows].astype(F32) + part[side, target, rows].astype(F32)
                    ).astype(BF16)
                    chain(side, way, k, False).start()

                if last == N_TP // 2:
                    one()
                else:
                    pl.when(k < N_TP // 2)(one)

        pl.when(is_dec)(lambda: go(1))
        go(0)
        for direction in range(2):
            def one_dots():
                chain_dots(direction, k - 1, True).wait_recv()
                rsd[direction, k - 2] = rsd[direction, k - 2] + dots[...]
                chain_dots(direction, k, False).start()

            if direction == 0:
                one_dots()
            else:
                pl.when(k < N_TP // 2)(one_dots)
        return 0

    def relay(side):
        give_far_mate(side).wait_recv()
        relay_mate(side).start()

    def settled(side):
        give_far(side).wait_recv()
        give_mate(side).wait_recv()
        relay_mate(side).wait_recv()
        keep_own(side).wait()

    def weight_gradient(w, side, out):
        for j in range(4):
            left_side = x_all[side, j].reshape(N_DP * ROWS, WIDE)
            right_side = g_all[w].reshape(N_DP * ROWS, WIDE)
            out[j] = dot_tn(left_side, right_side).astype(BF16)

    lax.fori_loop(2, 6, chain_step, 0)
    g_far().wait_recv()
    g_relay().start()
    relay(0)
    lax.fori_loop(6, 8, chain_step, 0)
    settled(0)
    g_mate().wait_recv()
    g_relay().wait_recv()
    g_keep.wait()
    weight_gradient(0, 0, dq_o)
    lax.fori_loop(8, N_TP // 2 + 1, chain_step, 0)
    chain_dots(0, N_TP // 2, True).wait_recv()
    chain_dots(1, N_TP // 2 - 1, True).wait_recv()
    summed = rsd[0, N_TP // 2 - 1] + rsd[1, N_TP // 2 - 2] + dots[...]

    def arrived(side, chunk):
        rows = pl.ds(chunk * HALF, HALF)
        total = part[side, z, rows].astype(F32)
        for direction in range(2):
            way = (direction, chunk)
            chain(side, way, hops(way), True).wait_recv()
            total = total + rs[side, direction, hops(way) - 1, rows].astype(F32)
        return total

    def column_of(side):
        across = jnp.broadcast_to(summed[0:1, side * 128 : (side + 1) * 128], (ROWS, ROWS))
        return jnp.sum(jnp.where(diagonal, across, 0.0), axis=1, keepdims=True)

    here = pl.ds(pl.multiple_of(z * WIDE, WIDE), WIDE)

    def give_memory(i):
        return remote(h_out.at[i], h_in.at[s - FIRST_DECODER], h_s.at[i], h_r.at[0], {"section": i})

    @pl.when(is_dec)
    def _():
        gain = fgain[0:1, here]
        column = column_of(1)
        for chunk in range(CHUNKS):
            rows = slice(chunk * HALF, (chunk + 1) * HALF)
            value = gain * arrived(1, chunk) - gat[1, z, rows].astype(F32) * column[rows]
            count = HALF // PIECE
            h_out[chunk * count : chunk * count + count] = value.reshape(count, PIECE, WIDE)
        for i in range(N_SECTION):
            @pl.when(s != i)
            def _():
                give_memory(i).start()
        pltpu.make_async_copy(h_out.at[s], h_in.at[s - FIRST_DECODER], h_r.at[0]).start()

    gain_here = lgain[0:1, here]
    stream_column = column_of(0)
    for chunk in range(CHUNKS):
        rows = slice(chunk * HALF, (chunk + 1) * HALF)
        value = gain_here * arrived(0, chunk) - stream[rows].astype(F32) * stream_column[rows]
        sg_o[rows] = value.astype(BF16)

    pl.when(is_dec)(lambda: relay(1))
    pl.when(is_dec)(lambda: settled(1))
    weight_gradient(1, src, dk_o)
    weight_gradient(2, src, dv_o)

    pltpu.make_async_copy(h_in, h_in, h_r.at[0]).wait()
    mg_o[...] = h_in[0] + h_in[1] + h_in[2] + h_in[3]

    def drain(which):
        for way in WAYS:
            def step(k, _):
                ring(which, way, k).wait_send()
                chain(which, way, k, True).wait_send()
                return 0

            lax.fori_loop(1, hops(way) + 1, step, 0)

    drain(0)
    pl.when(is_dec)(lambda: drain(1))
    for w in range(3):
        weight_mate(w).wait_send()
        for quarter in range(4 if w == 2 else 1):
            weight_far(w, quarter).wait_send()
            weight_relay(w, quarter).wait_send()
    for i in range(N_SECTION - FIRST_DECODER):
        @pl.when(s != FIRST_DECODER + i)
        def _():
            mem_send(i).wait_send()

    def drain_exchange(side):
        give_far(side).wait_send()
        give_far_mate(side).wait_send()
        give_mate(side).wait_send()
        relay_mate(side).wait_send()

    drain_exchange(0)
    pl.when(is_dec)(lambda: drain_exchange(1))
    g_far().wait_send()
    g_mate().wait_send()
    g_relay().wait_send()
    for direction in range(2):
        def step(k, _):
            chain_dots(direction, k, True).wait_send()
            return 0

        lax.fori_loop(1, N_TP // 2 + 1 - direction, step, 0)

    @pl.when(is_dec)
    def _():
        for i in range(N_SECTION):
            @pl.when(s != i)
            def _():
                give_memory(i).wait_send()


def hand_out(mix, sg, mg, dq, dk, dv, mix_o, sg_o, mg_o, dq_o, dk_o, dv_o):
    mix_o[...] = mix[...]
    sg_o[...] = sg[...]
    for n in range(4):
        mg_o[n] = mg[n * 4 : n * 4 + 4].astype(BF16)
    dq_o[...] = dq[...]
    dk_o[...] = dk[...]
    dv_o[...] = dv[...]


def shards(
    stream, memory_hidden, layer_gain, final_gain, query_weight, key_weight, value_weight,
    cotangent, encoder_lengths, decoder_lengths, assignment,
):
    vmem = pl.BlockSpec(memory_space=pltpu.VMEM)
    hbm = pl.BlockSpec(memory_space=pl.ANY)
    smem = pl.BlockSpec(memory_space=pltpu.SMEM)
    dma = pltpu.SemaphoreType.DMA
    outs = pl.pallas_call(
        body,
        name="relay",
        out_shape=(
            jax.ShapeDtypeStruct((ROWS, WIDE), BF16),
            jax.ShapeDtypeStruct((ROWS, WIDE), BF16),
            jax.ShapeDtypeStruct((PIECE, WIDE), F32),
            jax.ShapeDtypeStruct((4, WIDE, WIDE), BF16),
            jax.ShapeDtypeStruct((4, WIDE, WIDE), BF16),
            jax.ShapeDtypeStruct((4, WIDE, WIDE), BF16),
        ),
        in_specs=[vmem, vmem, vmem, vmem, hbm, hbm, hbm, vmem, smem, smem, smem],
        out_specs=(vmem,) * 6,
        scratch_shapes=[
            pltpu.VMEM((PIECE, WIDE), BF16),
            pltpu.VMEM((2, N_TP, ROWS, WIDE), BF16),
            pltpu.VMEM((2, N_TP, ROWS, WIDE), BF16),
            pltpu.VMEM((2, ROWS, WIDE), F32),
            pltpu.VMEM((3, N_TP, WIDE, WIDE), BF16),
            pltpu.VMEM((3, ROWS, WIDE), F32),
            pltpu.VMEM((2, ROWS, 128), F32),
            pltpu.VMEM((3, ROWS, WIDE), BF16),
            pltpu.VMEM((4, ROWS, ROWS), F32),
            pltpu.VMEM((ROWS, WIDE), BF16),
            pltpu.VMEM((3, ROWS, WIDE), BF16),
            pltpu.VMEM((3, N_DP, ROWS, WIDE), BF16),
            pltpu.VMEM((2, 4, N_DP, ROWS, WIDE), BF16),
            pltpu.VMEM((2, 4, ROWS, WIDE), BF16),
            pltpu.VMEM((2, N_TP, ROWS, WIDE), BF16),
            pltpu.VMEM((2, 2, N_TP // 2, ROWS, WIDE), BF16),
            pltpu.VMEM((8, 256), F32),
            pltpu.VMEM((2, N_TP // 2, 8, 256), F32),
            pltpu.VMEM((N_SECTION, PIECE, WIDE), F32),
            pltpu.VMEM((N_SECTION - FIRST_DECODER, PIECE, WIDE), F32),
            dma((2, 2, CHUNKS, 8)), dma((2, 2, CHUNKS, 8)),
            dma((6,)), dma((6,)), dma((3,)), dma((3,)), dma((6,)), dma((6,)),
            dma((4,)), dma((1,)),
            dma((3, 4)), dma((3, 4)),
            dma((2, 2, CHUNKS, 8)), dma((2, 2, CHUNKS, 8)),
            dma((2, 8)), dma((2, 8)),
            dma((8,)), dma((1,)),
            dma((7,)),
        ],
        compiler_params=pltpu.CompilerParams(
            collective_id=0, has_side_effects=True, vmem_limit_bytes=60 * 1024 * 1024
        ),
    )(
        stream.reshape(ROWS, WIDE),
        memory_hidden,
        layer_gain,
        final_gain.reshape(1, N_TP * WIDE),
        query_weight.reshape(4, WIDE, WIDE),
        key_weight.reshape(4, WIDE, WIDE),
        value_weight.reshape(4, WIDE, WIDE),
        cotangent.reshape(ROWS, WIDE),
        encoder_lengths,
        decoder_lengths,
        assignment.reshape(4),
    )
    mixture, stream_grad, memory_grad, dq, dk, dv = pl.pallas_call(
        hand_out,
        name="hand_out",
        out_shape=(
            jax.ShapeDtypeStruct((ROWS, WIDE), BF16),
            jax.ShapeDtypeStruct((ROWS, WIDE), BF16),
            jax.ShapeDtypeStruct((4, 4, WIDE), BF16),
            jax.ShapeDtypeStruct((4, WIDE, WIDE), BF16),
            jax.ShapeDtypeStruct((4, WIDE, WIDE), BF16),
            jax.ShapeDtypeStruct((4, WIDE, WIDE), BF16),
        ),
        in_specs=[vmem] * 6,
        out_specs=(vmem,) * 6,
    )(*outs)
    rows = (1, 4, 32, WIDE)
    square = (1, 4 * WIDE, WIDE)
    return (
        mixture.reshape(rows),
        stream_grad.reshape(rows),
        memory_grad,
        dq.reshape(square),
        dk.reshape(square),
        dv.reshape(square),
    )


def solution(mesh):
    tokens = P("section", "dp", None, "tp")
    weight = P("section", "dp", "tp")
    memory = P("dp", "section", "tp")
    return jax.shard_map(
        shards,
        mesh=mesh,
        in_specs=(
            tokens, memory, P("section", None), P(), weight, weight, weight, tokens, P("dp"), P("dp"), P("dp", None),
        ),
        out_specs=(tokens, tokens, memory, weight, weight, weight),
        check_vma=False,
    )
```
